128 devices in a mesh: fsdp: 16 (over y, z_hi, core), sp: 8 (over z_lo, x).
Axes of the slice: x: 4, y: 4, z: 4 (z_hi: 2, z_lo: 2; z = z_hi * 2 + z_lo), core: 2. Of those that a mesh axis runs over, the one named last changes fastest.
Arguments:
- tokens: bfloat16 [16384, 5120], P(('fsdp', 'sp')), may hold values from -6 to 6
- norm_gain: float32 [5120], replicated, may hold values from 0.1 to 1.9
- q_weight: bfloat16 [5120, 5120], P('fsdp', 'sp'), may hold values from -0.078125 to 0.078125
- key_matrix: bfloat16 [5120, 1024], P('fsdp', 'sp'), may hold values from -0.078125 to 0.078125
- value_matrix: bfloat16 [5120, 1024], P('fsdp', 'sp'), may hold values from -0.078125 to 0.078125
- q_bias: float32 [5120], P('sp'), may hold values from -8 to 8
- k_bias: float32 [1024], P('sp'), may hold values from -8 to 8
- value_offset_bias: float32 [1024], P('sp'), may hold values from -3 to 3
- out_weight: bfloat16 [5120, 5120], P('fsdp', 'sp'), may hold values from -0.078125 to 0.078125
Outputs:
- mixed: bfloat16 [16384, 5120], P(('fsdp', 'sp'))
The draws below stay inside these ranges and needn't reach their ends.
All inputs are finite; a program needn't handle non-finite values.
Results may differ from the reference program's by a relative error of at most 0.014.
Values may be sent and summed in bfloat16 or wider, within the bound.
A program may use at most 128 MiB of HBM per device.

```python
import jax
import jax.numpy as jnp
from jax import lax

MODEL_WIDTH = 5120
QUERY_HEADS = 40
KEY_VALUE_HEADS = 8
HEAD_SIZE = 128
SEQ_DEV = 128
TOKENS = 16384
HEAD_SETS = 8
N_FSDP = 16
N_SP = 8


def bias_pair(key):
    random_seed_key = jax.random.fold_in(key, 11)
    query_portion = jnp.clip(0.5 * jax.random.normal(jax.random.fold_in(random_seed_key, 3), (QUERY_HEADS * HEAD_SIZE,), jnp.float32), -8.0, 8.0)
    key_portion = jnp.clip(0.5 * jax.random.normal(jax.random.fold_in(random_seed_key, 4), (KEY_VALUE_HEADS * HEAD_SIZE,), jnp.float32), -8.0, 8.0)
    return (query_portion, key_portion)


def draw_q_bias(key, part):
    return bias_pair(key)[0]


def draw_k_bias(key, part):
    return bias_pair(key)[1]


def level_of(own_key, extent, cuts, least, high):
    def one(dim, shards_of):
        draws = jax.random.uniform(jax.random.fold_in(jax.random.fold_in(own_key, 6), dim), (shards_of,), jnp.float32, least / len(cuts), high / len(cuts))
        return jnp.repeat(jnp.exp(draws), extent[dim] // shards_of).reshape((-1,) + (1,) * (len(extent) - dim - 1))

    factor_of = one(*cuts[0])
    for cut in cuts[1:]:
        factor_of = factor_of * one(*cut)
    return factor_of


def scatter_about(rng, shape, scale, most, pieces=(), held_as=jnp.bfloat16):
    array = jax.random.normal(rng, shape, jnp.float32) * scale
    if len(pieces) > 0:
        array = level_of(rng, shape, pieces, -0.22, 0.18) * array
    return jnp.clip(array, min=-most, max=most).astype(held_as)


def setup_inputs(seed: int = 0) -> dict:
    arg_keys = jax.random.split(jax.random.key(seed), 10)
    tokens = scatter_about(arg_keys[0], (TOKENS, MODEL_WIDTH), 1.0, 6.0, ((0, 128),))
    norm_gain = jnp.clip(1.0 + 0.18 * jax.random.normal(arg_keys[1], (MODEL_WIDTH,), jnp.float32), 0.1, 1.9)
    q_weight = scatter_about(arg_keys[2], (MODEL_WIDTH, QUERY_HEADS * HEAD_SIZE), MODEL_WIDTH ** -0.5, 0.078125, ((0, 16), (1, 8)))
    key_matrix = scatter_about(arg_keys[3], (MODEL_WIDTH, KEY_VALUE_HEADS * HEAD_SIZE), MODEL_WIDTH ** -0.5, 0.078125, ((0, 16), (1, 8)))
    value_matrix = scatter_about(arg_keys[4], (MODEL_WIDTH, KEY_VALUE_HEADS * HEAD_SIZE), MODEL_WIDTH ** -0.5, 0.078125, ((0, 16), (1, 8)))
    q_bias = draw_q_bias(jax.random.fold_in(arg_keys[9], 71), 0)
    k_bias = draw_k_bias(jax.random.fold_in(arg_keys[9], 71), 0)
    value_offset_bias = scatter_about(arg_keys[7], (KEY_VALUE_HEADS * HEAD_SIZE,), 0.5, 3.0, ((0, 8),), jnp.float32)
    out_weight = scatter_about(arg_keys[8], (MODEL_WIDTH, QUERY_HEADS * HEAD_SIZE), (QUERY_HEADS * HEAD_SIZE) ** -0.5, 0.078125, ((0, 16), (1, 8)))
    return dict(tokens=tokens, norm_gain=norm_gain, q_weight=q_weight, key_matrix=key_matrix, value_matrix=value_matrix, q_bias=q_bias, k_bias=k_bias, value_offset_bias=value_offset_bias, out_weight=out_weight)


ROPE_BASE = 1000000.0

def rms_normed(tokens, norm_gain):
    rows = tokens.astype(jnp.float32)
    meansq = lax.optimization_barrier(jnp.mean(rows * rows, axis=-1, keepdims=True))
    return (rows * lax.rsqrt(meansq + 1e-06) * norm_gain).astype(jnp.bfloat16)

def rotary(projected, positions):
    count = projected.shape[0]
    heads_grid = projected.reshape(count, -1, HEAD_SIZE)
    half_dim = HEAD_SIZE // 2
    frequency = ROPE_BASE ** (-(jnp.arange(half_dim, dtype=jnp.float32) * 2.0 / HEAD_SIZE))
    angle = positions[:, None] * frequency[None, :]
    cosine = jnp.cos(angle)[:, None, :]
    sine = jnp.sin(angle)[:, None, :]
    first = heads_grid[..., :half_dim]
    second = heads_grid[..., half_dim:]
    rotated = jnp.concatenate([first * cosine - second * sine, second * cosine + first * sine], axis=-1)
    return rotated.reshape(count, -1)

def attend(queries, keys, values):
    length = queries.shape[0]
    kv_heads = keys.shape[1] // HEAD_SIZE
    group_size = queries.shape[1] // keys.shape[1]
    query_grid = queries.reshape(length, kv_heads, group_size, HEAD_SIZE).astype(jnp.float32)
    key_grid = keys.reshape(length, kv_heads, HEAD_SIZE).astype(jnp.float32)
    value_grid = values.reshape(length, kv_heads, HEAD_SIZE).astype(jnp.float32)
    scores = jnp.einsum('qkgd,skd->kgqs', query_grid, key_grid) / jnp.sqrt(jnp.float32(HEAD_SIZE))
    causal = jnp.arange(length)[:, None] >= jnp.arange(length)[None, :]
    scores = jnp.where(causal, scores, jnp.float32(-1e+30))
    largest = lax.optimization_barrier(jnp.max(scores, axis=-1, keepdims=True))
    weights = jnp.exp(scores - largest)
    totals = lax.optimization_barrier(jnp.sum(weights, axis=-1, keepdims=True))
    probs = (weights / totals).astype(jnp.bfloat16)
    result = jnp.einsum('kgqs,skd->qkgd', probs.astype(jnp.float32), value_grid)
    return result.reshape(length, -1).astype(jnp.bfloat16)

def reference(tokens, norm_gain, q_weight, key_matrix, value_matrix, q_bias, k_bias, value_offset_bias, out_weight):
    length = SEQ_DEV * N_SP
    positions = jnp.arange(length, dtype=jnp.float32)
    set_cols = QUERY_HEADS * HEAD_SIZE // HEAD_SETS
    out_sets = out_weight.reshape(MODEL_WIDTH, HEAD_SETS, set_cols).transpose(1, 0, 2)

    def one_sequence(rows):
        normed = rms_normed(rows, norm_gain)
        queries = rotary(jnp.dot(normed, q_weight, preferred_element_type=jnp.float32) + q_bias, positions).astype(jnp.bfloat16)
        keys = rotary(jnp.dot(normed, key_matrix, preferred_element_type=jnp.float32) + k_bias, positions).astype(jnp.bfloat16)
        values = (jnp.dot(normed, value_matrix, preferred_element_type=jnp.float32) + value_offset_bias).astype(jnp.bfloat16)
        heads = attend(queries, keys, values)
        head_sets = heads.reshape(length, HEAD_SETS, set_cols).transpose(1, 0, 2)

        def add_set(total, pair):
            term = jnp.dot(pair[0], pair[1].T, preferred_element_type=jnp.float32).astype(jnp.bfloat16)
            return (total + term.astype(jnp.float32), 0)
        total, unused = lax.scan(add_set, jnp.zeros((length, MODEL_WIDTH), jnp.float32), (head_sets, out_sets))
        return total.astype(jnp.bfloat16)
    mixed = lax.map(one_sequence, tokens.reshape(N_FSDP, length, MODEL_WIDTH))
    return mixed.reshape(N_FSDP * length, MODEL_WIDTH)
```

```python
import functools

import jax
import jax.numpy as jnp
import numpy as np
from jax import lax
from jax.experimental import pallas as pl
from jax.experimental.pallas import tpu as pltpu
from jax.sharding import PartitionSpec as P

MESH = pl.DeviceIdType.MESH
WIDTH = 5120
HEAD = 128
GROUP = 5
QC = GROUP * HEAD
WC = QC + 2 * HEAD
SEQ = 1024
ROWS = 128
WR = 320
HR = WR // 2
KC = 1280
NK = WIDTH // KC
OC = 640
NO = WIDTH // OC
N_SEND = 260
F32 = jnp.float32
BF16 = jnp.bfloat16


def rope_tables():
    half = HEAD // 2
    freq = np.float32(1000000.0) ** (-(np.arange(half, dtype=np.float32) * 2.0 / HEAD)).astype(np.float32)
    angle = (np.arange(SEQ, dtype=np.float32)[:, None] * freq[None, :]).astype(np.float64)
    cos = np.cos(angle).astype(np.float32)
    sin = np.sin(angle).astype(np.float32)
    return np.concatenate([cos, cos], 1), np.concatenate([-sin, sin], 1)


def kernel(
    tok_hbm, gain, wq_hbm, wk_hbm, wv_hbm, bq_in, bk_in, bv_in, wo_hbm, cos_hbm, sin_hbm,
    out,
    tok, stage, xb, wb, wob, acc, qb, kb, vb, hb, cosb, sinb, bq, bk, bv,
    prcv, r1, r2, held,
    lsem, ssem, wsem, wosem, wsib, xsem, xsib, swsem, bsem, psem, r1sem, r2sem, fsem,
):
    f = lax.axis_index("fsdp")
    s = lax.axis_index("sp")
    c = f % 2
    zh = (f // 2) % 2
    y = f // 4
    zl = s // 4
    x = s % 4
    z = zh * 2 + zl
    home = c == zl
    away = c != zl
    yp, ym, y2 = (y + 1) % 4, (y + 3) % 4, (y + 2) % 4
    zp, zm, z2 = (z + 1) % 4, (z + 3) % 4, (z + 2) % 4
    xp, xm, x2 = (x + 1) % 4, (x + 3) % 4, (x + 2) % 4

    def dev(y_, z_, x_, c_):
        return ((y_ * 2 + z_ // 2) * 2 + c_, (z_ % 2) * 4 + x_)

    YP, YM = dev(yp, z, x, c), dev(ym, z, x, c)
    ZP, ZM = dev(y, zp, x, c), dev(y, zm, x, c)
    XP, XM = dev(y, z, xp, c), dev(y, z, xm, c)
    SIB = dev(y, z, x, 1 - c)
    SWAP = dev(y, zh * 2 + c, x, zl)

    sends = []

    def send(mk, cond=None):
        k = len(sends)
        mk(ssem.at[k]).start()
        sends.append((cond, mk))

    def wait_sends(lo, hi):
        for cond in (None, home, away):
            group = [(k, sends[k][1]) for k in range(lo, hi) if sends[k][0] is cond]
            if not group:
                continue

            def drain(group=group):
                for k, mk in group:
                    mk(ssem.at[k]).wait_send()

            if cond is None:
                drain()
            else:
                pl.when(cond)(drain)

    def remote(refs, to):
        def mk(sem):
            src, dst, rsem = refs()
            return pltpu.make_async_remote_copy(
                src_ref=src, dst_ref=dst, send_sem=sem, recv_sem=rsem, device_id=to, device_id_type=MESH
            )

        return mk

    def wait_recv(dst, rsem):
        pltpu.make_async_remote_copy(
            src_ref=dst, dst_ref=dst, send_sem=ssem.at[0], recv_sem=rsem, device_id=SIB, device_id_type=MESH
        ).wait_recv()

    pltpu.make_async_copy(tok_hbm, tok, lsem.at[0]).start()
    barrier = pltpu.get_barrier_semaphore()
    for peer in (YP, YM, ZP, ZM, XP, XM, SIB):
        pl.semaphore_signal(barrier, inc=1, device_id=peer, device_id_type=MESH)

    @pl.when(away)
    def _():
        pl.semaphore_signal(barrier, inc=1, device_id=SWAP, device_id_type=MESH)

    pltpu.make_async_copy(cos_hbm, cosb, lsem.at[1]).start()
    pltpu.make_async_copy(sin_hbm, sinb, lsem.at[2]).start()

    def block(y_, z_, i):
        return (y_, z_, i)

    def index_of(b):
        return 4 * b[0] + 2 * (b[1] // 2) + b[2]

    own_f = index_of((y, z, c))
    sib_f = index_of((y, z, 1 - c))

    def own_rows(buf, f_):
        return buf.at[pl.ds(pl.multiple_of(f_ * WR, 32), WR)]

    local_parts = (
        (wq_hbm, wb, 0, QC), (wk_hbm, wb, QC, HEAD), (wv_hbm, wb, QC + HEAD, HEAD), (wo_hbm, wob, 0, QC),
    )

    def part_view(buf, f_, col, n):
        return buf.at[pl.ds(pl.multiple_of(f_ * WR, 32), WR), pl.ds(col, n)]

    @pl.when(home)
    def _():
        for k, (src, buf, col, n) in enumerate(local_parts):
            pltpu.make_async_copy(src, part_view(buf, own_f, col, n), lsem.at[3 + k]).start()
        for k, (src, dst) in enumerate(((bq_in, bq), (bk_in, bk), (bv_in, bv))):
            dst[...] = src[...]

    pltpu.make_async_copy(tok_hbm, tok, lsem.at[0]).wait()
    my_rows = pl.multiple_of(c * (4 * ROWS) + x * ROWS, ROWS)

    def norm_to(dst, base):
        @pl.loop(0, ROWS // 16)
        def _(r):
            r0 = pl.multiple_of(r * 16, 16)
            t = tok[pl.ds(r0, 16), :].astype(F32)
            ms = jnp.mean(t * t, axis=-1, keepdims=True)
            dst[pl.ds(pl.multiple_of(base + r0, 16), 16), :] = (t * lax.rsqrt(ms + 1e-06) * gain[...]).astype(BF16)

    @pl.when(home)
    def _():
        norm_to(xb, my_rows)

    @pl.when(away)
    def _():
        norm_to(stage, 0)

    pl.semaphore_wait(barrier, 7 + (1 - (c == zl).astype(jnp.int32)))

    class Flow:
        def __init__(self, buf, rsem):
            self.buf, self.rsem = buf, rsem

        def refs(self, b, h):
            k = index_of(b)
            v = self.buf.at[pl.ds(pl.multiple_of(k * WR + h * HR, 32), HR)]
            return v, v, self.rsem.at[k, h]

        def fwd(self, b, h, to, cond):
            send(remote(lambda: self.refs(b, h), to), cond)

        def wait(self, b, h):
            _, v, sem = self.refs(b, h)
            wait_recv(v, sem)

        def h0(self):
            for h in (0, 1):
                for to in (YP, YM):
                    self.fwd(block(y, z, 1), h, to, home)
                for to in (ZP, ZM):
                    self.fwd(block(y, z, 0), h, to, home)
            for h in (0, 1):
                for to in (YP, YM):
                    self.fwd(block(y, z, 0), h, to, home)
                for to in (ZP, ZM):
                    self.fwd(block(y, z, 1), h, to, home)

        def relay_y(self, z_, i, cond):
            self.wait(block(ym, z_, i), 0)
            self.fwd(block(ym, z_, i), 0, YP, cond)
            self.wait(block(yp, z_, i), 1)
            self.fwd(block(yp, z_, i), 1, YM, cond)
            self.wait(block(ym, z_, i), 1)
            self.wait(block(yp, z_, i), 0)

        def relay_z(self, y_, i, cond):
            self.wait(block(y_, zm, i), 0)
            self.fwd(block(y_, zm, i), 0, ZP, cond)
            self.wait(block(y_, zp, i), 1)
            self.fwd(block(y_, zp, i), 1, ZM, cond)
            self.wait(block(y_, zm, i), 1)
            self.wait(block(y_, zp, i), 0)

        def both(self, f_, dirs, cond):
            for h in (0, 1):
                for to in dirs:
                    self.fwd(f_, h, to, cond)

        def h1(self):
            self.relay_y(z, 1, home)
            self.both(block(ym, z, 1), (ZP, ZM), home)
            self.both(block(yp, z, 1), (ZP, ZM), home)

        def h2(self):
            self.relay_y(z, 0, home)

        def take(self, f_):
            self.wait(f_, 0)
            self.wait(f_, 1)

        def h3(self):
            self.take(block(y2, z, 1))
            self.both(block(y2, z, 1), (ZP, ZM), home)

        def h4(self):
            self.take(block(y, z2, 0))
            self.both(block(y, z2, 0), (YP, YM), home)
            self.take(block(y, z2, 1))

        def h5(self):
            self.relay_y(z2, 0, home)

        def h6(self):
            self.take(block(ym, z2, 1))
            self.take(block(yp, z2, 1))

        def h7(self):
            self.take(block(y2, z, 0))
            self.take(block(y2, z2, 0))
            self.take(block(y2, z2, 1))

        def n1(self):
            self.relay_z(y, 0, away)
            self.both(block(y, zm, 0), (YP, YM), away)
            self.both(block(y, zp, 0), (YP, YM), away)

        def n2(self):
            self.relay_z(y, 1, away)

        def n3(self):
            self.relay_y(zm, 0, away)
            self.relay_y(zp, 0, away)

        def n4(self):
            self.relay_z(ym, 1, away)
            self.relay_z(yp, 1, away)

        def n5(self):
            self.relay_z(y2, 1, away)

        def n6(self):
            self.take(block(y2, zm, 0))
            self.take(block(y2, zp, 0))

        def step(self, h=(), n=()):
            if h:
                @pl.when(home)
                def _():
                    for name in h:
                        getattr(self, name)()
            if n:
                @pl.when(away)
                def _():
                    for name in n:
                        getattr(self, name)()

    qkv = Flow(wb, wsem)
    wout = Flow(wob, wosem)

    def place(parts, h_flow):
        @pl.when(away)
        def _():
            for k, (src, buf, col, n) in parts:
                send(remote(lambda a=src, b=buf, o=col, m=n, k=k: (a, part_view(b, own_f, o, m), wsib.at[k]), SIB), away)

        @pl.when(home)
        def _():
            for k, (src, buf, col, n) in parts:
                pltpu.make_async_copy(src, part_view(buf, own_f, col, n), lsem.at[3 + k]).wait()
                wait_recv(part_view(buf, sib_f, col, n), wsib.at[k])
            h_flow.h0()

    enum_parts = list(enumerate(local_parts))

    chunk_at = (y, yp, ym, y2)

    def xv(core, x_, kk, r0=0, nr=ROWS):
        return xb.at[
            pl.ds(pl.multiple_of(core * (4 * ROWS) + x_ * ROWS + r0, 16), nr),
            pl.ds(pl.multiple_of(chunk_at[kk] * KC, 128), KC),
        ]

    def x_swap():
        @pl.when(away)
        def _():
            for kk in range(NK):
                send(remote(lambda kk=kk: (
                    stage.at[:, pl.ds(pl.multiple_of(chunk_at[kk] * KC, 128), KC)], xv(1 - c, x, kk), swsem.at[kk]
                ), SWAP), away)
                if kk == 0:
                    for k, (a, b) in enumerate(((bq_in, bq), (bk_in, bk), (bv_in, bv))):
                        send(remote(lambda a=a, b=b, k=k: (a, b, bsem.at[k]), SWAP), away)

    half_rows = ROWS // 2

    def xsend(where, sem, to):
        def refs():
            v = xv(*where)
            return v, v, sem

        send(remote(refs, to))

    def x_own(kk):
        @pl.when(away)
        def _():
            wait_recv(xv(c, x, kk), swsem.at[kk])

        xsend((c, x, kk), xsem.at[kk, 0], XP)
        xsend((c, x, kk), xsem.at[kk, 1], XM)
        xsend((c, x, kk), xsib.at[kk, 0], SIB)

    def x_relay(kk):
        wait_recv(xv(c, xm, kk), xsem.at[kk, 0])
        xsend((c, xm, kk, 0, half_rows), xsem.at[kk, 2], XP)
        wait_recv(xv(c, xp, kk), xsem.at[kk, 1])
        xsend((c, xp, kk, half_rows, half_rows), xsem.at[kk, 3], XM)
        xsend((c, xm, kk), xsib.at[kk, 1], SIB)
        xsend((c, xp, kk), xsib.at[kk, 2], SIB)

    def x_last(kk):
        wait_recv(xv(c, x2, kk, 0, half_rows), xsem.at[kk, 2])
        wait_recv(xv(c, x2, kk, half_rows, half_rows), xsem.at[kk, 3])
        xsend((c, x2, kk), xsib.at[kk, 3], SIB)

    def x_sib(kk):
        for k, x_ in enumerate((x, xm, xp, x2)):
            wait_recv(xv(1 - c, x_, kk), xsib.at[kk, k])

    RB = 256

    def project(kk):
        cols = pl.ds(pl.multiple_of(chunk_at[kk] * KC, 128), KC)

        @pl.loop(0, SEQ // RB)
        def _(r):
            rows = pl.ds(pl.multiple_of(r * RB, RB), RB)
            d = jnp.dot(xb[rows, cols], wb[cols, :], preferred_element_type=F32)
            if kk == 0:
                acc[rows, :] = d
            else:
                acc[rows, :] += d

    x_swap()
    place(enum_parts[:3], qkv)
    x_own(0)
    x_own(1)
    qkv.step(h=("h1",), n=("n1",))
    x_relay(0)
    qkv.step(h=("h2",), n=("n2",))
    x_own(2)
    x_last(0)
    qkv.step(h=("h3", "h4"))
    x_relay(1)
    x_own(3)
    x_sib(0)
    project(0)
    x_last(1)
    qkv.step(h=("h5",), n=("n3", "n4"))
    x_relay(2)
    x_sib(1)
    x_last(2)
    x_sib(2)
    qkv.step(h=("h6",), n=("n5",))
    place(enum_parts[3:], wout)
    project(1)
    x_relay(3)
    project(2)
    x_last(3)
    qkv.step(h=("h7",), n=("n6",))
    x_sib(3)
    project(3)
    wout.step(h=("h1",), n=("n1",))

    pltpu.make_async_copy(cos_hbm, cosb, lsem.at[1]).wait()
    pltpu.make_async_copy(sin_hbm, sinb, lsem.at[2]).wait()

    @pl.when(away)
    def _():
        for k, b in enumerate((bq, bk, bv)):
            wait_recv(b, bsem.at[k])

    @pl.loop(0, SEQ // 128)
    def _(r):
        rows = pl.ds(pl.multiple_of(r * 128, 128), 128)
        cs, sn = cosb[rows, :], sinb[rows, :]
        for h in range(GROUP + 1):
            col = slice(h * HEAD, (h + 1) * HEAD)
            bias = bq[:, col] if h < GROUP else bk[...]
            t = acc[rows, col] + bias
            t = (t * cs + pltpu.roll(t, HEAD // 2, 1) * sn).astype(BF16)
            if h < GROUP:
                qb[rows, col] = t
            else:
                kb[rows, :] = t
        vb[rows, :] = (acc[rows, QC + HEAD :] + bv[...]).astype(BF16)

    scale = 1.0 / float(np.sqrt(np.float32(HEAD)))
    QB = 256

    def attend(i):
        n = (i + 1) * QB

        @pl.loop(0, GROUP)
        def _(h):
            col = pl.ds(pl.multiple_of(h * HEAD, HEAD), HEAD)
            q = qb[i * QB : n, col]
            sc = lax.dot_general(q, kb[:n, :], (((1,), (1,)), ((), ())), preferred_element_type=F32) * scale
            qi = lax.broadcasted_iota(jnp.int32, (QB, n), 0) + i * QB
            ki = lax.broadcasted_iota(jnp.int32, (QB, n), 1)
            sc = jnp.where(qi >= ki, sc, -1e30)
            w = jnp.exp(sc - jnp.max(sc, axis=-1, keepdims=True))
            tot = jnp.sum(w, axis=-1, keepdims=True)
            o = jnp.dot(w.astype(BF16), vb[:n, :], preferred_element_type=F32)
            hb[i * QB : n, col] = (o / tot).astype(BF16)

    attend(0)
    wout.step(h=("h2",), n=("n2",))
    attend(1)
    wout.step(h=("h3", "h4"))
    attend(2)
    attend(3)

    n_phase1 = len(sends)
    wait_sends(0, n_phase1)

    def st(r0, nr, j):
        return xb.at[pl.ds(r0, nr), pl.ds(j * OC, OC)]

    def out_at(j):
        ky, k2 = chunk_at[j // 2], j % 2
        return (ky * 2 + k2) * OC

    def terms(j):
        wrow = pl.ds(pl.multiple_of(out_at(j), 128), OC)

        def dot(row):
            return lax.dot_general(
                hb[pl.ds(pl.multiple_of(row, 128), 256), :], wob[wrow, :], (((1,), (1,)), ((), ())),
                preferred_element_type=F32,
            )

        @pl.loop(0, 2)
        def _(r):
            xb[pl.ds(pl.multiple_of(r * 256, 256), 256), pl.ds(j * OC, OC)] = dot((1 - c) * 512 + r * 256).astype(BF16)

        send(remote(lambda: (st(0, 512, j), prcv.at[j], psem.at[j]), SIB))

        @pl.loop(0, 2)
        def _(r):
            acc[pl.ds(pl.multiple_of((j % 2) * 512 + r * 256, 256), 256), pl.ds(0, OC)] = dot(c * 512 + r * 256)

    def pair(j):
        wait_recv(prcv.at[j], psem.at[j])
        oc = pl.ds(j * OC, OC)

        def total(x_, h):
            r0 = x_ * ROWS + h * half_rows
            mine = acc[pl.ds(pl.multiple_of((j % 2) * 512 + r0, 64), half_rows), pl.ds(0, OC)]
            return mine + prcv[j, pl.ds(pl.multiple_of(r0, 64), half_rows), :].astype(F32)

        for h in (0, 1):
            xb[512 + h * 64 : 576 + h * 64, oc] = total(x2, h).astype(BF16)
        send(remote(lambda: (st(512, 64, j), r1.at[j, 0], r1sem.at[j, 0]), XP))
        send(remote(lambda: (st(576, 64, j), r1.at[j, 1], r1sem.at[j, 1]), XM))
        xb[704:768, oc] = total(xp, 1).astype(BF16)
        xb[768:832, oc] = total(xm, 0).astype(BF16)
        send(remote(lambda: (st(704, 64, j), r2.at[j, 1], r2sem.at[j, 1]), XP))
        send(remote(lambda: (st(768, 64, j), r2.at[j, 2], r2sem.at[j, 2]), XM))
        held[j, 0] = total(xp, 0)
        held[j, 1] = total(xm, 1)
        held[j, 2] = total(x, 0)
        held[j, 3] = total(x, 1)

    def relay(j):
        oc = pl.ds(j * OC, OC)
        wait_recv(r1.at[j, 0], r1sem.at[j, 0])
        xb[640:704, oc] = (held[j, 0] + r1[j, 0].astype(F32)).astype(BF16)
        send(remote(lambda: (st(640, 64, j), r2.at[j, 0], r2sem.at[j, 0]), XP))
        wait_recv(r1.at[j, 1], r1sem.at[j, 1])
        xb[832:896, oc] = (held[j, 1] + r1[j, 1].astype(F32)).astype(BF16)
        send(remote(lambda: (st(832, 64, j), r2.at[j, 3], r2sem.at[j, 3]), XM))

    def out_cols(j):
        return pl.ds(pl.multiple_of(out_at(j), 128), OC)

    def final(j):
        oc = pl.ds(j * OC, OC)
        for k in range(4):
            wait_recv(r2.at[j, k], r2sem.at[j, k])

        def whole(h):
            return (held[j, 2 + h] + r2[j, h].astype(F32) + r2[j, 2 + h].astype(F32)).astype(BF16)

        @pl.when(home)
        def _():
            for h in (0, 1):
                out[h * 64 : h * 64 + 64, out_cols(j)] = whole(h)

        @pl.when(away)
        def _():
            for h in (0, 1):
                xb[896 + h * 64 : 960 + h * 64, oc] = whole(h)
            send(remote(lambda: (st(896, 128, j), out.at[:, out_cols(j)], fsem.at[j]), SWAP), away)

    for it in range(NO + 3):
        if it == 2:
            wout.step(h=("h5",), n=("n3", "n4"))
            wout.step(h=("h6",))
        if it == 4:
            wout.step(n=("n5",))
        if it == 6:
            wout.step(h=("h7",), n=("n6",))
        if it < NO:
            terms(it)
        if 0 <= it - 1 < NO:
            pair(it - 1)
        if 0 <= it - 2 < NO:
            relay(it - 2)
        if 0 <= it - 3 < NO:
            final(it - 3)

    @pl.when(away)
    def _():
        for j in range(NO):
            wait_recv(out.at[:, out_cols(j)], fsem.at[j])

    wait_sends(n_phase1, len(sends))
    assert len(sends) <= N_SEND, len(sends)


def body(tokens, gain, wq, wk, wv, bq, bk, bv, wo):
    cos, sin = rope_tables()
    any_, vm = pl.BlockSpec(memory_space=pl.ANY), pl.BlockSpec(memory_space=pltpu.VMEM)
    dma = lambda *n: pltpu.SemaphoreType.DMA(n)
    return pl.pallas_call(
        kernel,
        out_shape=jax.ShapeDtypeStruct((ROWS, WIDTH), BF16),
        in_specs=[any_, vm, any_, any_, any_, vm, vm, vm, any_, any_, any_],
        out_specs=vm,
        scratch_shapes=[
            pltpu.VMEM((ROWS, WIDTH), BF16),
            pltpu.VMEM((ROWS, WIDTH), BF16),
            pltpu.VMEM((SEQ, WIDTH), BF16),
            pltpu.VMEM((WIDTH, WC), BF16),
            pltpu.VMEM((WIDTH, QC), BF16),
            pltpu.VMEM((SEQ, WC), F32),
            pltpu.VMEM((SEQ, QC), BF16),
            pltpu.VMEM((SEQ, HEAD), BF16),
            pltpu.VMEM((SEQ, HEAD), BF16),
            pltpu.VMEM((SEQ, QC), BF16),
            pltpu.VMEM((SEQ, HEAD), F32),
            pltpu.VMEM((SEQ, HEAD), F32),
            pltpu.VMEM((1, QC), F32),
            pltpu.VMEM((1, HEAD), F32),
            pltpu.VMEM((1, HEAD), F32),
            pltpu.VMEM((NO, 512, OC), BF16),
            pltpu.VMEM((NO, 2, 64, OC), BF16),
            pltpu.VMEM((NO, 4, 64, OC), BF16),
            pltpu.VMEM((NO, 4, 64, OC), F32),
            dma(8), dma(N_SEND), dma(16, 2), dma(16, 2), dma(4), dma(NK, 4), dma(NK, 4), dma(NK), dma(3),
            dma(NO), dma(NO, 2), dma(NO, 4), dma(NO),
        ],
        compiler_params=pltpu.CompilerParams(
            collective_id=0, has_side_effects=True, vmem_limit_bytes=67043328
        ),
    )(
        tokens, gain.reshape(1, -1), wq, wk, wv, bq.reshape(1, -1), bk.reshape(1, -1), bv.reshape(1, -1), wo,
        jnp.asarray(cos), jnp.asarray(sin),
    )


def solution(mesh):
    placed = (
        P(("fsdp", "sp"), None), P(), P("fsdp", "sp"), P("fsdp", "sp"), P("fsdp", "sp"),
        P("sp"), P("sp"), P("sp"), P("fsdp", "sp"),
    )
    return jax.shard_map(
        body, mesh=mesh, in_specs=placed, out_specs=P(("fsdp", "sp"), None), check_vma=False
    )
```

```python
import functools

import jax
import jax.numpy as jnp
import numpy as np
from jax import lax
from jax.experimental import pallas as pl
from jax.experimental.pallas import tpu as pltpu
from jax.sharding import PartitionSpec as P

MESH = pl.DeviceIdType.MESH
WIDTH = 5120
HEAD = 128
GROUP = 5
QC = GROUP * HEAD
WC = QC + 2 * HEAD
SEQ = 1024
ROWS = 128
WR = 320
HR = WR // 2
KC = 1280
NK = WIDTH // KC
OC = 640
NO = WIDTH // OC
N_SEND = 300
F32 = jnp.float32
BF16 = jnp.bfloat16
LATE_Q, OUTER_Q = 0, (0, 2)
LATE_O, OUTER_O = 1, (0, 2, 3)
SCHEDULE = (
    "qo", "xw", "xo0", "qn1", "xr0", "xo1", "xo2", "qs", "qh1", "qh3", "qh2", "qn2", "xl0", "wo", "xo3", "xr1",
    "qh4", "xr2", "qn4a", "xl1", "qh5", "xl2", "xs0", "xs1", "ws", "xr3", "qh4b", "p00", "qn4b", "qn3a", "wh1", "xs2",
    "p01", "qn3b", "p20", "qn5", "qh7b", "xl3", "p10", "qh7a", "qh6", "p11", "p21", "qn6b", "qn6a", "xs3", "p30", "wn1",
    "qh8", "p31", "e", "a302", "wn2", "a325", "a105", "a005", "d", "a202", "wh4b", "t00", "a225", "wn4a", "t10", "g10",
    "g00", "r00", "wn4b", "wn3a", "wh3", "r10", "wh2", "wh4", "t12", "g12", "t14", "g14", "f00", "t02", "r12", "g02",
    "t11", "t04", "wn5", "g11", "wn6a", "g04", "wh7a", "t16", "t01", "g01", "wh6", "wn3b", "g16", "t06", "f10", "g06",
    "wh5", "t03", "t13", "r01", "r04", "r06", "g03", "wh7b", "t05", "r02", "wh8", "r11", "r14", "r16", "g05", "g13",
    "t15", "wn6b", "t07", "r13", "f11", "g15", "t17", "f12", "r03", "f06", "g07", "f04", "f01", "f13", "f02", "r05",
    "f16", "g17", "r07", "f03", "r15", "f05", "r17", "f07", "f14", "f15", "f17",
)


def rope_tables():
    half = HEAD // 2
    freq = np.float32(1000000.0) ** (-(np.arange(half, dtype=np.float32) * 2.0 / HEAD)).astype(np.float32)
    angle = (np.arange(SEQ, dtype=np.float32)[:, None] * freq[None, :]).astype(np.float64)
    cos = np.cos(angle).astype(np.float32)
    sin = np.sin(angle).astype(np.float32)
    return np.concatenate([cos, sin], 1)


def kernel(
    tok_hbm, gain, wq_hbm, wk_hbm, wv_hbm, bq_in, bk_in, bv_in, wo_hbm, trig_hbm,
    out,
    tok, stage, xb, wb, wob, acc, qb, kb, vb, hb, trig, bq, bk, bv,
    prcv, r1, r2, held,
    lsem, ssem, wsem, wosem, wsib, xsem, xsib, swsem, bsem, psem, r1sem, r2sem, fsem,
):
    f = lax.axis_index("fsdp")
    s = lax.axis_index("sp")
    c = f % 2
    zh = (f // 2) % 2
    y = f // 4
    zl = s // 4
    x = s % 4
    z = zh * 2 + zl
    home = c == zl
    away = c != zl
    cores = (c == 0, c == 1)
    aways = ((c == 0) & away, (c == 1) & away)
    yp, ym, y2 = (y + 1) % 4, (y + 3) % 4, (y + 2) % 4
    zp, zm, z2 = (z + 1) % 4, (z + 3) % 4, (z + 2) % 4
    xp, xm, x2 = (x + 1) % 4, (x + 3) % 4, (x + 2) % 4

    def dev(y_, z_, x_, c_):
        return ((y_ * 2 + z_ // 2) * 2 + c_, (z_ % 2) * 4 + x_)

    YP, YM = dev(yp, z, x, c), dev(ym, z, x, c)
    ZP, ZM = dev(y, zp, x, c), dev(y, zm, x, c)
    XP, XM = dev(y, z, xp, c), dev(y, z, xm, c)
    SIB = dev(y, z, x, 1 - c)
    SWAP = dev(y, zh * 2 + c, x, zl)

    sends, token = [], [None]

    def send(mk, cond=None):
        k = len(sends)
        mk(ssem.at[k]).start()
        sends.append((cond, mk, token[0]))

    def wait_sends(of_tokens):
        for cond in (None, home, away, *cores, *aways):
            group = [(k, e[1]) for k, e in enumerate(sends) if e[0] is cond and (e[2] == "x") == of_tokens]
            if not group:
                continue

            def drain(group=group):
                for k, mk in group:
                    mk(ssem.at[k]).wait_send()

            if cond is None:
                drain()
            else:
                pl.when(cond)(drain)

    def remote(refs, to):
        def mk(sem):
            src, dst, rsem = refs()
            return pltpu.make_async_remote_copy(
                src_ref=src, dst_ref=dst, send_sem=sem, recv_sem=rsem, device_id=to, device_id_type=MESH
            )

        return mk

    def wait_recv(dst, rsem):
        pltpu.make_async_remote_copy(
            src_ref=dst, dst_ref=dst, send_sem=ssem.at[0], recv_sem=rsem, device_id=SIB, device_id_type=MESH
        ).wait_recv()

    pltpu.make_async_copy(tok_hbm, tok, lsem.at[0]).start()
    barrier = pltpu.get_barrier_semaphore()
    for peer in (YP, YM, ZP, ZM, XP, XM, SIB):
        pl.semaphore_signal(barrier, inc=1, device_id=peer, device_id_type=MESH)

    @pl.when(away)
    def _():
        pl.semaphore_signal(barrier, inc=1, device_id=SWAP, device_id_type=MESH)

    pltpu.make_async_copy(trig_hbm, trig, lsem.at[1]).start()

    def block(y_, z_, i):
        return (y_, z_, i)

    def index_of(b):
        return 4 * b[0] + 2 * (b[1] // 2) + b[2]

    own_f = index_of((y, z, c))
    sib_f = index_of((y, z, 1 - c))

    def own_rows(buf, f_):
        return buf.at[pl.ds(pl.multiple_of(f_ * WR, 32), WR)]

    local_parts = (
        (wq_hbm, wb, 0, QC), (wk_hbm, wb, QC, HEAD), (wv_hbm, wb, QC + HEAD, HEAD), (wo_hbm, wob, 0, QC),
    )

    def part_view(buf, f_, col, n):
        return buf.at[pl.ds(pl.multiple_of(f_ * WR, 32), WR), pl.ds(col, n)]

    @pl.when(home)
    def _():
        for k, (src, buf, col, n) in enumerate(local_parts):
            pltpu.make_async_copy(src, part_view(buf, own_f, col, n), lsem.at[3 + k]).start()
        for k, (src, dst) in enumerate(((bq_in, bq), (bk_in, bk), (bv_in, bv))):
            dst[...] = src[...]

    pltpu.make_async_copy(tok_hbm, tok, lsem.at[0]).wait()
    my_rows = pl.multiple_of(c * (4 * ROWS) + x * ROWS, ROWS)

    def norm_to(dst, base):
        @pl.loop(0, ROWS // 16)
        def _(r):
            r0 = pl.multiple_of(r * 16, 16)
            t = tok[pl.ds(r0, 16), :].astype(F32)
            ms = jnp.mean(t * t, axis=-1, keepdims=True)
            dst[pl.ds(pl.multiple_of(base + r0, 16), 16), :] = (t * lax.rsqrt(ms + 1e-06) * gain[...]).astype(BF16)

    @pl.when(home)
    def _():
        norm_to(xb, my_rows)

    @pl.when(away)
    def _():
        norm_to(stage, 0)

    pl.semaphore_wait(barrier, 7 + (c + zl) % 2)

    zq, zn = z + 1 - 2 * zl, (z + 3 + 2 * zl) % 4
    ZN = dev(y, zn, x, c)

    class Flow:
        def __init__(self, buf, rsem, late, outer):
            self.buf, self.rsem = buf, rsem
            self.own = [(0, 0), (0, 1)]
            self.sib = [(1, 0), (1, 1)]
            self.zfirst = self.sib + self.own[2 - late :]
            self.yfirst = self.own[: 2 - late]
            self.outer = outer

        def refs(self, y_, z_, u):
            k = 4 * y_ + 2 * (z_ // 2) + (c + u[0]) % 2
            v = self.buf.at[pl.ds(pl.multiple_of(k * WR + u[1] * HR, 32), HR)]
            return v, v, self.rsem.at[k, u[1]]

        def fwd(self, y_, z_, u, to, cond):
            send(remote(lambda: self.refs(y_, z_, u), to), cond)

        def wait(self, y_, z_, units):
            for u in units:
                _, v, sem = self.refs(y_, z_, u)
                wait_recv(v, sem)

        def spread(self, y_, z_, units, dirs, cond):
            for u in units:
                for to in dirs:
                    self.fwd(y_, z_, u, to, cond)

        def relay_y(self, z_, units, flip, cond):
            for n, u in enumerate(units):
                for y_, to, turn in ((ym, YP, 0), (yp, YM, 1)):
                    self.wait(y_, z_, [u])
                    if (n + flip) % 2 == turn:
                        self.fwd(y_, z_, u, to, cond)

        def relay_z(self, y_, units, row, cond):
            for n, u in enumerate(units):
                if row in self.outer:
                    self.wait(y_, zq, [u])
                    self.fwd(y_, zq, u, ZN, cond)
                    self.wait(y_, zn, [u])
                    continue
                for z_, to, turn in ((zm, ZP, 0), (zp, ZM, 1)):
                    self.wait(y_, z_, [u])
                    if n % 2 == turn:
                        self.fwd(y_, z_, u, to, cond)

        def h0(self):
            for u in self.own:
                self.spread(y, z, [u], (YP, YM, ZP, ZM), home)

        def h0s(self):
            for u in self.sib:
                self.spread(y, z, [u], (ZP, ZM, YP, YM), home)

        def h1(self):
            self.relay_y(z, self.yfirst, 0, home)
            self.spread(ym, z, self.yfirst, (ZP, ZM), home)
            self.spread(yp, z, self.yfirst, (ZP, ZM), home)

        def h2(self):
            self.relay_y(z, self.zfirst, len(self.yfirst), home)

        def h3(self):
            self.wait(y2, z, self.yfirst)
            self.spread(y2, z, self.yfirst, (ZP, ZM), home)

        def h4(self):
            for u in self.zfirst[::-1]:
                self.wait(y, z2, [u])
                self.spread(y, z2, [u], (YP, YM), home)

        def h4b(self):
            self.wait(y, z2, self.yfirst)

        def h5(self):
            self.relay_y(z2, self.zfirst[::-1], 0, home)

        def h6(self):
            self.wait(ym, z2, self.yfirst)
            self.wait(yp, z2, self.yfirst)

        def h7a(self):
            self.wait(y2, z, self.zfirst)

        def h7b(self):
            self.wait(y2, z2, self.zfirst)

        def h8(self):
            self.wait(y2, z2, self.yfirst)

        def n1(self):
            self.relay_z(y, self.own, 0, away)
            u = self.own[2 - len(self.zfirst) + 2 :]
            for v in u:
                for z_ in (zm, zp):
                    self.spread(y, z_, [v], (YP, YM), away)

        def n2(self):
            self.relay_z(y, self.sib, 1, away)
            for v in self.sib:
                for z_ in (zm, zp):
                    self.spread(y, z_, [v], (YP, YM), away)

        def n3a(self):
            self.relay_y(zq, self.order_n(), 0, away)

        def n3b(self):
            self.relay_y(zn, self.order_n(), 1, away)

        def order_n(self):
            return [u for u in self.zfirst if u[0] == 0] + self.sib

        def n4a(self):
            self.relay_z(ym, self.yfirst, 2, away)

        def n4b(self):
            self.relay_z(yp, self.yfirst, 3, away)

        def n5(self):
            self.relay_z(y2, self.yfirst, 4, away)

        def n6a(self):
            self.wait(y2, zq, self.zfirst)

        def n6b(self):
            self.wait(y2, zn, self.zfirst)

        def step(self, name):
            @pl.when(home if name[0] == "h" else away)
            def _():
                getattr(self, name)()

    qkv = Flow(wb, wsem, LATE_Q, OUTER_Q)
    wout = Flow(wob, wosem, LATE_O, OUTER_O)

    def place_own(parts, flow):
        @pl.when(away)
        def _():
            for k, (src, buf, col, n) in parts:
                send(remote(lambda a=src, b=buf, o=col, m=n, k=k: (a, part_view(b, own_f, o, m), wsib.at[k]), SIB), away)

        @pl.when(home)
        def _():
            for k, (src, buf, col, n) in parts:
                pltpu.make_async_copy(src, part_view(buf, own_f, col, n), lsem.at[3 + k]).wait()
            flow.h0()

    def place_sib(parts, flow):
        @pl.when(home)
        def _():
            for k, (src, buf, col, n) in parts:
                wait_recv(part_view(buf, sib_f, col, n), wsib.at[k])
            flow.h0s()

    parts_of = {"q": list(enumerate(local_parts))[:3], "w": list(enumerate(local_parts))[3:]}

    chunk_at = (y, yp, ym, y2)

    def xv(core, x_, kk, r0=0, nr=ROWS):
        return xb.at[
            pl.ds(pl.multiple_of(core * (4 * ROWS) + x_ * ROWS + r0, 16), nr),
            pl.ds(pl.multiple_of(chunk_at[kk] * KC, 128), KC),
        ]

    def x_swap():
        @pl.when(away)
        def _():
            for kk in range(NK):
                send(remote(lambda kk=kk: (
                    stage.at[:, pl.ds(pl.multiple_of(chunk_at[kk] * KC, 128), KC)], xv(1 - c, x, kk), swsem.at[kk]
                ), SWAP), away)
                if kk == 0:
                    for k, (a, b) in enumerate(((bq_in, bq), (bk_in, bk), (bv_in, bv))):
                        send(remote(lambda a=a, b=b, k=k: (a, b, bsem.at[k]), SWAP), away)

    half_rows = ROWS // 2

    def xsend(where, sem, to):
        def refs():
            v = xv(*where)
            return v, v, sem

        send(remote(refs, to))

    def x_own(kk):
        @pl.when(away)
        def _():
            wait_recv(xv(c, x, kk), swsem.at[kk])

        xsend((c, x, kk), xsem.at[kk, 0], XP)
        xsend((c, x, kk), xsem.at[kk, 1], XM)
        xsend((c, x, kk), xsib.at[kk, 0], SIB)

    def x_relay(kk):
        wait_recv(xv(c, xm, kk), xsem.at[kk, 0])
        xsend((c, xm, kk, 0, half_rows), xsem.at[kk, 2], XP)
        wait_recv(xv(c, xp, kk), xsem.at[kk, 1])
        xsend((c, xp, kk, half_rows, half_rows), xsem.at[kk, 3], XM)
        xsend((c, xm, kk), xsib.at[kk, 1], SIB)
        xsend((c, xp, kk), xsib.at[kk, 2], SIB)

    def x_last(kk):
        wait_recv(xv(c, x2, kk, 0, half_rows), xsem.at[kk, 2])
        wait_recv(xv(c, x2, kk, half_rows, half_rows), xsem.at[kk, 3])
        xsend((c, x2, kk), xsib.at[kk, 3], SIB)

    def x_sib(kk):
        for k, x_ in enumerate((x, xm, xp, x2)):
            wait_recv(xv(1 - c, x_, kk), xsib.at[kk, k])

    RB = 256

    def feature_block(kk, side):
        return (chunk_at[kk] * 2 + (zh + side) % 2) * OC

    started = []

    def project(kk, side):
        cols = pl.ds(pl.multiple_of(feature_block(kk, side), 128), OC)
        first = not started
        started.append(kk)

        @pl.loop(0, SEQ // RB)
        def _(r):
            rows = pl.ds(pl.multiple_of(r * RB, RB), RB)
            d = jnp.dot(xb[rows, cols], wb[cols, :], preferred_element_type=F32)
            if first:
                acc[rows, :] = d
            else:
                acc[rows, :] += d

    def rope():
        pltpu.make_async_copy(trig_hbm, trig, lsem.at[1]).wait()

        @pl.when(away)
        def _():
            for k, b in enumerate((bq, bk, bv)):
                wait_recv(b, bsem.at[k])

        @pl.loop(0, SEQ // 128)
        def _(r):
            rows = pl.ds(pl.multiple_of(r * 128, 128), 128)
            here = trig[rows, :]
            other = pltpu.roll(here, HEAD // 2, 1)
            low = lax.broadcasted_iota(jnp.int32, (128, HEAD), 1) < HEAD // 2
            cs, sn = jnp.where(low, here, other), jnp.where(low, -other, here)
            for h in range(GROUP + 1):
                col = slice(h * HEAD, (h + 1) * HEAD)
                bias = bq[col][None, :] if h < GROUP else bk[...]
                t = acc[rows, col] + bias
                t = (t * cs + pltpu.roll(t, HEAD // 2, 1) * sn).astype(BF16)
                if h < GROUP:
                    qb[rows, col] = t
                else:
                    kb[rows, :] = t
            vb[rows, :] = (acc[rows, QC + HEAD :] + bv[...]).astype(BF16)

    scale = float(np.log2(np.e)) / float(np.sqrt(HEAD))
    QB = 256

    def attend(i, lo, hi):
        n = (i + 1) * QB

        @pl.loop(lo, hi, unroll=hi - lo)
        def _(h):
            col = pl.ds(pl.multiple_of(h * HEAD, HEAD), HEAD)
            q = qb[i * QB : n, col]
            near, far = slice(i * QB, n), slice(0, i * QB)

            def score(part):
                return lax.dot_general(q, kb[part, :], (((1,), (1,)), ((), ())), preferred_element_type=F32)

            qi = lax.broadcasted_iota(jnp.int32, (QB, QB), 0)
            ki = lax.broadcasted_iota(jnp.int32, (QB, QB), 1)
            parts = [(near, jnp.where(qi >= ki, score(near), -1e30))] + ([(far, score(far))] if i else [])
            top = functools.reduce(jnp.maximum, [jnp.max(sc, axis=-1, keepdims=True) for _, sc in parts])
            tot, o = 0.0, 0.0
            for part, sc in parts:
                w = jnp.exp2((sc - top) * scale)
                tot += jnp.sum(w, axis=-1, keepdims=True)
                o += jnp.dot(w.astype(BF16), vb[part, :], preferred_element_type=F32)
            hb[near, col] = (o / tot).astype(BF16)

    def st(r0, nr, j):
        return xb.at[pl.ds(r0, nr), pl.ds(j * OC, OC)]

    def out_at(j):
        return feature_block(j // 2, j % 2)

    def terms(st_, j):
        wrow = pl.ds(pl.multiple_of(out_at(j), 128), OC)

        @pl.loop(0, 2)
        def _(r):
            rows = pl.ds(pl.multiple_of(st_ * 512 + r * 256, 256), 256)
            acc[rows, pl.ds(0, OC)] = lax.dot_general(
                hb[rows, :], wob[wrow, :], (((1,), (1,)), ((), ())), preferred_element_type=F32
            )

        @pl.when(c != st_)
        def _():
            @pl.loop(0, 8)
            def _(r):
                r0 = pl.multiple_of(r * 64, 64)
                xb[pl.ds(r0, 64), pl.ds(j * OC, OC)] = acc[pl.ds(st_ * 512 + r0, 64), pl.ds(0, OC)].astype(BF16)

            send(remote(lambda: (st(0, 512, j), prcv.at[j], psem.at[j]), SIB), cores[1 - st_])

    def pair(st_, j, mine_):
        wait_recv(prcv.at[j], psem.at[j])
        oc = pl.ds(j * OC, OC)

        def total(x_, h):
            r0 = x_ * ROWS + h * half_rows
            mine = acc[pl.ds(pl.multiple_of(st_ * 512 + r0, 64), half_rows), pl.ds(0, OC)]
            return mine + prcv[j, pl.ds(pl.multiple_of(r0, 64), half_rows), :].astype(F32)

        for h in (0, 1):
            xb[512 + h * 64 : 576 + h * 64, oc] = total(x2, h).astype(BF16)
        send(remote(lambda: (st(512, 64, j), r1.at[j, 0], r1sem.at[j, 0]), XP), mine_)
        send(remote(lambda: (st(576, 64, j), r1.at[j, 1], r1sem.at[j, 1]), XM), mine_)
        xb[704:768, oc] = total(xp, 1).astype(BF16)
        xb[768:832, oc] = total(xm, 0).astype(BF16)
        send(remote(lambda: (st(704, 64, j), r2.at[j, 1], r2sem.at[j, 1]), XP), mine_)
        send(remote(lambda: (st(768, 64, j), r2.at[j, 2], r2sem.at[j, 2]), XM), mine_)
        held[j, 0] = total(xp, 0)
        held[j, 1] = total(xm, 1)
        held[j, 2] = total(x, 0)
        held[j, 3] = total(x, 1)

    def relay(st_, j, mine_):
        oc = pl.ds(j * OC, OC)
        wait_recv(r1.at[j, 0], r1sem.at[j, 0])
        xb[640:704, oc] = (held[j, 0] + r1[j, 0].astype(F32)).astype(BF16)
        send(remote(lambda: (st(640, 64, j), r2.at[j, 0], r2sem.at[j, 0]), XP), mine_)
        wait_recv(r1.at[j, 1], r1sem.at[j, 1])
        xb[832:896, oc] = (held[j, 1] + r1[j, 1].astype(F32)).astype(BF16)
        send(remote(lambda: (st(832, 64, j), r2.at[j, 3], r2sem.at[j, 3]), XM), mine_)

    def out_cols(j):
        return pl.ds(pl.multiple_of(out_at(j), 128), OC)

    def final(st_, j, mine_):
        oc = pl.ds(j * OC, OC)
        for k in range(4):
            wait_recv(r2.at[j, k], r2sem.at[j, k])

        def whole(h):
            return (held[j, 2 + h] + r2[j, h].astype(F32) + r2[j, 2 + h].astype(F32)).astype(BF16)

        @pl.when(home)
        def _():
            for h in (0, 1):
                out[h * 64 : h * 64 + 64, out_cols(j)] = whole(h)

        @pl.when(away)
        def _():
            for h in (0, 1):
                xb[896 + h * 64 : 960 + h * 64, oc] = whole(h)
            send(remote(lambda: (st(896, 128, j), out.at[:, out_cols(j)], fsem.at[j]), SWAP), aways[st_])

    def ring(fn, st_, j):
        pl.when(cores[st_])(lambda: fn(st_, j, cores[st_]))

    for tok_ in SCHEDULE:
        kind, arg = tok_[0], tok_[1:]
        token[0] = kind
        if kind == "x":
            {"w": x_swap, "o": x_own, "r": x_relay, "l": x_last, "s": x_sib}[arg[0]](*map(int, arg[1:]))
        elif kind in "qw" and arg == "o":
            place_own(parts_of[kind], qkv if kind == "q" else wout)
        elif kind in "qw" and arg == "s":
            place_sib(parts_of[kind], qkv if kind == "q" else wout)
        elif kind in "qw":
            (qkv if kind == "q" else wout).step(arg)
        elif kind == "p":
            project(*map(int, arg))
        elif kind == "e":
            rope()
        elif kind == "a":
            attend(*map(int, arg))
        elif kind == "d":
            wait_sends(True)
        elif kind == "t":
            terms(*map(int, arg))
        else:
            ring({"g": pair, "r": relay, "f": final}[kind], *map(int, arg))

    @pl.when(away)
    def _():
        for j in range(NO):
            wait_recv(out.at[:, out_cols(j)], fsem.at[j])

    wait_sends(False)
    assert len(sends) <= N_SEND, len(sends)


def body(tokens, gain, wq, wk, wv, bq, bk, bv, wo):
    trig = rope_tables()
    any_, vm = pl.BlockSpec(memory_space=pl.ANY), pl.BlockSpec(memory_space=pltpu.VMEM)
    dma = lambda *n: pltpu.SemaphoreType.DMA(n)
    return pl.pallas_call(
        kernel,
        out_shape=jax.ShapeDtypeStruct((ROWS, WIDTH), BF16),
        in_specs=[any_, vm, any_, any_, any_, vm, vm, vm, any_, any_],
        out_specs=vm,
        scratch_shapes=[
            pltpu.VMEM((ROWS, WIDTH), BF16),
            pltpu.VMEM((ROWS, WIDTH), BF16),
            pltpu.VMEM((SEQ, WIDTH), BF16),
            pltpu.VMEM((WIDTH, WC), BF16),
            pltpu.VMEM((WIDTH, QC), BF16),
            pltpu.VMEM((SEQ, WC), F32),
            pltpu.VMEM((SEQ, QC), BF16),
            pltpu.VMEM((SEQ, HEAD), BF16),
            pltpu.VMEM((SEQ, HEAD), BF16),
            pltpu.VMEM((SEQ, QC), BF16),
            pltpu.VMEM((SEQ, HEAD), F32),
            pltpu.VMEM((QC,), F32),
            pltpu.VMEM((1, HEAD), F32),
            pltpu.VMEM((1, HEAD), F32),
            pltpu.VMEM((NO, 512, OC), BF16),
            pltpu.VMEM((NO, 2, 64, OC), BF16),
            pltpu.VMEM((NO, 4, 64, OC), BF16),
            pltpu.VMEM((NO, 4, 64, OC), F32),
            dma(8), dma(N_SEND), dma(16, 2), dma(16, 2), dma(4), dma(NK, 4), dma(NK, 4), dma(NK), dma(3),
            dma(NO), dma(NO, 2), dma(NO, 4), dma(NO),
        ],
        compiler_params=pltpu.CompilerParams(
            collective_id=0, has_side_effects=True, vmem_limit_bytes=67043328
        ),
    )(
        tokens, gain.reshape(1, -1), wq, wk, wv, bq, bk.reshape(1, -1), bv.reshape(1, -1), wo,
        jnp.asarray(trig),
    )


def solution(mesh):
    placed = (
        P(("fsdp", "sp"), None), P(), P("fsdp", "sp"), P("fsdp", "sp"), P("fsdp", "sp"),
        P("sp"), P("sp"), P("sp"), P("fsdp", "sp"),
    )
    return jax.shard_map(
        body, mesh=mesh, in_specs=placed, out_specs=P(("fsdp", "sp"), None), check_vma=False
    )
```

```python
import functools

import jax
import jax.numpy as jnp
import numpy as np
from jax import lax
from jax.experimental import pallas as pl
from jax.experimental.pallas import tpu as pltpu
from jax.sharding import PartitionSpec as P

MESH = pl.DeviceIdType.MESH
WIDTH = 5120
HEAD = 128
GROUP = 5
QC = GROUP * HEAD
WC = QC + 2 * HEAD
SEQ = 1024
ROWS = 128
WR = 320
HR = WR // 2
KC = 1280
NK = WIDTH // KC
OC = 640
NO = WIDTH // OC
N_SEND = 300
F32 = jnp.float32
BF16 = jnp.bfloat16
LATE_Q, OUTER_Q = 0, (0, 1)
LATE_O, OUTER_O = 1, (0, 1, 2, 3)
SCHEDULE = (
    "qo", "n", "qn1", "xw", "xo0", "qs", "qn2", "xo1", "xo2", "qh1", "xr0", "qn4a", "qh2", "xr1", "xr2", "xo3",
    "qh3", "qn3b", "wo", "qh4", "xl0", "xs0", "qn4b", "qh4b", "qn3a", "xl2", "p00", "xl1", "xr3", "ws", "p01", "xs2",
    "p20", "qh6", "xs1", "qn5", "wh1", "qh5", "p11", "xl3", "p10", "qn6b", "wh2", "p21", "qh7a", "xs3", "qn6a", "p30",
    "wn1", "qh7b", "qh8", "p31", "e", "d", "a202", "wn2", "a325", "wh3", "a302", "a225", "t10", "a005", "a105", "t00",
    "g00", "wn4a", "g10", "wn3a", "wn4b", "t02", "wh7a", "r10", "t12", "g12", "wh4b", "t14", "wh4", "g14", "g02", "wn3b",
    "t11", "r00", "wn5", "t04", "g11", "r02", "wn6a", "t16", "f00", "g04", "t01", "g01", "t06", "g06", "f02", "f10",
    "wh6", "wh5", "t03", "r14", "r12", "g16", "wh8", "wn6b", "t13", "r04", "g13", "t15", "g15", "f14", "r01", "g03",
    "t05", "wh7b", "t17", "f12", "g17", "f04", "f01", "r03", "g05", "t07", "g07", "r16", "r06", "r13", "r17", "f16",
    "r15", "f03", "r11", "f13", "r05", "r07", "f17", "f15", "f06", "f05", "f07", "f11",
)


def rope_tables():
    half = HEAD // 2
    freq = np.float32(1000000.0) ** (-(np.arange(half, dtype=np.float32) * 2.0 / HEAD)).astype(np.float32)
    angle = (np.arange(SEQ, dtype=np.float32)[:, None] * freq[None, :]).astype(np.float64)
    cos = np.cos(angle).astype(np.float32)
    sin = np.sin(angle).astype(np.float32)
    return np.concatenate([cos, sin], 1)


def kernel(
    tok_hbm, gain, wq_hbm, wk_hbm, wv_hbm, bq_in, bk_in, bv_in, wo_hbm, trig_hbm,
    out,
    tok, stage, xb, wb, wob, acc, qb, kb, vb, hb, trig, bq, bk, bv,
    prcv, r1, r2, held,
    lsem, ssem, wsem, wosem, wsib, xsem, xsib, swsem, bsem, psem, r1sem, r2sem, fsem,
):
    f = lax.axis_index("fsdp")
    s = lax.axis_index("sp")
    c = f % 2
    zh = (f // 2) % 2
    y = f // 4
    zl = s // 4
    x = s % 4
    z = zh * 2 + zl
    home = c == zl
    away = c != zl
    cores = (c == 0, c == 1)
    aways = ((c == 0) & away, (c == 1) & away)
    yp, ym, y2 = (y + 1) % 4, (y + 3) % 4, (y + 2) % 4
    zp, zm, z2 = (z + 1) % 4, (z + 3) % 4, (z + 2) % 4
    xp, xm, x2 = (x + 1) % 4, (x + 3) % 4, (x + 2) % 4

    def dev(y_, z_, x_, c_):
        return ((y_ * 2 + z_ // 2) * 2 + c_, (z_ % 2) * 4 + x_)

    YP, YM = dev(yp, z, x, c), dev(ym, z, x, c)
    ZP, ZM = dev(y, zp, x, c), dev(y, zm, x, c)
    XP, XM = dev(y, z, xp, c), dev(y, z, xm, c)
    SIB = dev(y, z, x, 1 - c)
    SWAP = dev(y, zh * 2 + c, x, zl)

    sends, token = [], [None]

    def send(mk, cond=None):
        k = len(sends)
        mk(ssem.at[k]).start()
        sends.append((cond, mk, token[0]))

    def wait_sends(of_tokens):
        for cond in (None, home, away, *cores, *aways):
            group = [(k, e[1]) for k, e in enumerate(sends) if e[0] is cond and (e[2] == "x") == of_tokens]
            if not group:
                continue

            def drain(group=group):
                for k, mk in group:
                    mk(ssem.at[k]).wait_send()

            if cond is None:
                drain()
            else:
                pl.when(cond)(drain)

    def remote(refs, to):
        def mk(sem):
            src, dst, rsem = refs()
            return pltpu.make_async_remote_copy(
                src_ref=src, dst_ref=dst, send_sem=sem, recv_sem=rsem, device_id=to, device_id_type=MESH
            )

        return mk

    def wait_recv(dst, rsem):
        pltpu.make_async_remote_copy(
            src_ref=dst, dst_ref=dst, send_sem=ssem.at[0], recv_sem=rsem, device_id=SIB, device_id_type=MESH
        ).wait_recv()

    pltpu.make_async_copy(tok_hbm, tok, lsem.at[0]).start()
    barrier = pltpu.get_barrier_semaphore()
    for peer in (YP, YM, ZP, ZM, XP, XM, SIB):
        pl.semaphore_signal(barrier, inc=1, device_id=peer, device_id_type=MESH)

    @pl.when(away)
    def _():
        pl.semaphore_signal(barrier, inc=1, device_id=SWAP, device_id_type=MESH)

    pltpu.make_async_copy(trig_hbm, trig, lsem.at[1]).start()

    def block(y_, z_, i):
        return (y_, z_, i)

    def index_of(b):
        return 4 * b[0] + 2 * (b[1] // 2) + b[2]

    own_f = index_of((y, z, c))
    sib_f = index_of((y, z, 1 - c))

    def own_rows(buf, f_):
        return buf.at[pl.ds(pl.multiple_of(f_ * WR, 32), WR)]

    local_parts = (
        (wq_hbm, wb, 0, QC), (wk_hbm, wb, QC, HEAD), (wv_hbm, wb, QC + HEAD, HEAD), (wo_hbm, wob, 0, QC),
    )

    def part_view(buf, f_, col, n):
        return buf.at[pl.ds(pl.multiple_of(f_ * WR, 32), WR), pl.ds(col, n)]

    @pl.when(home)
    def _():
        for k, (src, buf, col, n) in enumerate(local_parts):
            pltpu.make_async_copy(src, part_view(buf, own_f, col, n), lsem.at[3 + k]).start()
        for k, (src, dst) in enumerate(((bq_in, bq), (bk_in, bk), (bv_in, bv))):
            dst[...] = src[...]

    my_rows = pl.multiple_of(c * (4 * ROWS) + x * ROWS, ROWS)

    def norm_to(dst, base):
        @pl.loop(0, ROWS // 16)
        def _(r):
            r0 = pl.multiple_of(r * 16, 16)
            t = tok[pl.ds(r0, 16), :].astype(F32)
            ms = jnp.mean(t * t, axis=-1, keepdims=True)
            dst[pl.ds(pl.multiple_of(base + r0, 16), 16), :] = (t * lax.rsqrt(ms + 1e-06) * gain[...]).astype(BF16)

    def norm():
        pltpu.make_async_copy(tok_hbm, tok, lsem.at[0]).wait()

        @pl.when(home)
        def _():
            norm_to(xb, my_rows)

        @pl.when(away)
        def _():
            norm_to(stage, 0)

    pl.semaphore_wait(barrier, 7 + (c + zl) % 2)

    zq, zn = z + 1 - 2 * zl, (z + 3 + 2 * zl) % 4
    ZN = dev(y, zn, x, c)

    class Flow:
        def __init__(self, buf, rsem, late, outer):
            self.buf, self.rsem = buf, rsem
            self.own = [(0, 0), (0, 1)]
            self.sib = [(1, 0), (1, 1)]
            self.zfirst = self.sib + self.own[2 - late :]
            self.yfirst = self.own[: 2 - late]
            self.outer = outer

        def refs(self, y_, z_, u):
            k = 4 * y_ + 2 * (z_ // 2) + (c + u[0]) % 2
            v = self.buf.at[pl.ds(pl.multiple_of(k * WR + u[1] * HR, 32), HR)]
            return v, v, self.rsem.at[k, u[1]]

        def fwd(self, y_, z_, u, to, cond):
            send(remote(lambda: self.refs(y_, z_, u), to), cond)

        def wait(self, y_, z_, units):
            for u in units:
                _, v, sem = self.refs(y_, z_, u)
                wait_recv(v, sem)

        def spread(self, y_, z_, units, dirs, cond):
            for u in units:
                for to in dirs:
                    self.fwd(y_, z_, u, to, cond)

        def relay_y(self, z_, units, flip, cond):
            for n, u in enumerate(units):
                for y_, to, turn in ((ym, YP, 0), (yp, YM, 1)):
                    self.wait(y_, z_, [u])
                    if (n + flip) % 2 == turn:
                        self.fwd(y_, z_, u, to, cond)

        def relay_z(self, y_, units, row, cond):
            for n, u in enumerate(units):
                if row in self.outer:
                    self.wait(y_, zq, [u])
                    self.fwd(y_, zq, u, ZN, cond)
                    self.wait(y_, zn, [u])
                    continue
                for z_, to, turn in ((zm, ZP, 0), (zp, ZM, 1)):
                    self.wait(y_, z_, [u])
                    if n % 2 == turn:
                        self.fwd(y_, z_, u, to, cond)

        def h0(self):
            for u in self.own:
                self.spread(y, z, [u], (YP, YM, ZP, ZM), home)

        def h0s(self):
            for u in self.sib:
                self.spread(y, z, [u], (ZP, ZM, YP, YM), home)

        def h1(self):
            self.relay_y(z, self.yfirst, 0, home)
            self.spread(ym, z, self.yfirst, (ZP, ZM), home)
            self.spread(yp, z, self.yfirst, (ZP, ZM), home)

        def h2(self):
            self.relay_y(z, self.zfirst, len(self.yfirst), home)

        def h3(self):
            self.wait(y2, z, self.yfirst)
            self.spread(y2, z, self.yfirst, (ZP, ZM), home)

        def h4(self):
            for u in self.zfirst[::-1]:
                self.wait(y, z2, [u])
                self.spread(y, z2, [u], (YP, YM), home)

        def h4b(self):
            self.wait(y, z2, self.yfirst)

        def h5(self):
            self.relay_y(z2, self.zfirst[::-1], 0, home)

        def h6(self):
            self.wait(ym, z2, self.yfirst)
            self.wait(yp, z2, self.yfirst)

        def h7a(self):
            self.wait(y2, z, self.zfirst)

        def h7b(self):
            self.wait(y2, z2, self.zfirst)

        def h8(self):
            self.wait(y2, z2, self.yfirst)

        def n1(self):
            self.relay_z(y, self.own, 0, away)
            u = self.own[2 - len(self.zfirst) + 2 :]
            for v in u:
                for z_ in (zm, zp):
                    self.spread(y, z_, [v], (YP, YM), away)

        def n2(self):
            self.relay_z(y, self.sib, 1, away)
            for v in self.sib:
                for z_ in (zm, zp):
                    self.spread(y, z_, [v], (YP, YM), away)

        def n3a(self):
            self.relay_y(zq, self.order_n(), 0, away)

        def n3b(self):
            self.relay_y(zn, self.order_n(), 1, away)

        def order_n(self):
            return [u for u in self.zfirst if u[0] == 0] + self.sib

        def n4a(self):
            self.relay_z(ym, self.yfirst, 2, away)

        def n4b(self):
            self.relay_z(yp, self.yfirst, 3, away)

        def n5(self):
            self.relay_z(y2, self.yfirst, 4, away)

        def n6a(self):
            self.wait(y2, zq, self.zfirst)

        def n6b(self):
            self.wait(y2, zn, self.zfirst)

        def step(self, name):
            @pl.when(home if name[0] == "h" else away)
            def _():
                getattr(self, name)()

    qkv = Flow(wb, wsem, LATE_Q, OUTER_Q)
    wout = Flow(wob, wosem, LATE_O, OUTER_O)

    def place_own(parts, flow):
        @pl.when(away)
        def _():
            for k, (src, buf, col, n) in parts:
                send(remote(lambda a=src, b=buf, o=col, m=n, k=k: (a, part_view(b, own_f, o, m), wsib.at[k]), SIB), away)

        @pl.when(home)
        def _():
            for k, (src, buf, col, n) in parts:
                pltpu.make_async_copy(src, part_view(buf, own_f, col, n), lsem.at[3 + k]).wait()
            flow.h0()

    def place_sib(parts, flow):
        @pl.when(home)
        def _():
            for k, (src, buf, col, n) in parts:
                wait_recv(part_view(buf, sib_f, col, n), wsib.at[k])
            flow.h0s()

    parts_of = {"q": list(enumerate(local_parts))[:3], "w": list(enumerate(local_parts))[3:]}

    chunk_at = (y, yp, ym, y2)

    def xv(core, x_, kk, r0=0, nr=ROWS):
        return xb.at[
            pl.ds(pl.multiple_of(core * (4 * ROWS) + x_ * ROWS + r0, 16), nr),
            pl.ds(pl.multiple_of(chunk_at[kk] * KC, 128), KC),
        ]

    def x_swap():
        @pl.when(away)
        def _():
            for kk in range(NK):
                send(remote(lambda kk=kk: (
                    stage.at[:, pl.ds(pl.multiple_of(chunk_at[kk] * KC, 128), KC)], xv(1 - c, x, kk), swsem.at[kk]
                ), SWAP), away)
                if kk == 0:
                    for k, (a, b) in enumerate(((bq_in, bq), (bk_in, bk), (bv_in, bv))):
                        send(remote(lambda a=a, b=b, k=k: (a, b, bsem.at[k]), SWAP), away)

    half_rows = ROWS // 2

    def xsend(where, sem, to):
        def refs():
            v = xv(*where)
            return v, v, sem

        send(remote(refs, to))

    def x_own(kk):
        @pl.when(away)
        def _():
            wait_recv(xv(c, x, kk), swsem.at[kk])

        xsend((c, x, kk), xsem.at[kk, 0], XP)
        xsend((c, x, kk), xsem.at[kk, 1], XM)
        xsend((c, x, kk), xsib.at[kk, 0], SIB)

    def x_relay(kk):
        wait_recv(xv(c, xm, kk), xsem.at[kk, 0])
        xsend((c, xm, kk, 0, half_rows), xsem.at[kk, 2], XP)
        wait_recv(xv(c, xp, kk), xsem.at[kk, 1])
        xsend((c, xp, kk, half_rows, half_rows), xsem.at[kk, 3], XM)
        xsend((c, xm, kk), xsib.at[kk, 1], SIB)
        xsend((c, xp, kk), xsib.at[kk, 2], SIB)

    def x_last(kk):
        wait_recv(xv(c, x2, kk, 0, half_rows), xsem.at[kk, 2])
        wait_recv(xv(c, x2, kk, half_rows, half_rows), xsem.at[kk, 3])
        xsend((c, x2, kk), xsib.at[kk, 3], SIB)

    def x_sib(kk):
        for k, x_ in enumerate((x, xm, xp, x2)):
            wait_recv(xv(1 - c, x_, kk), xsib.at[kk, k])

    RB = 256

    def feature_block(kk, side):
        return (chunk_at[kk] * 2 + (zh + side) % 2) * OC

    started = []

    def project(kk, side):
        cols = pl.ds(pl.multiple_of(feature_block(kk, side), 128), OC)
        first = not started
        started.append(kk)

        @pl.loop(0, SEQ // RB)
        def _(r):
            rows = pl.ds(pl.multiple_of(r * RB, RB), RB)
            d = jnp.dot(xb[rows, cols], wb[cols, :], preferred_element_type=F32)
            if first:
                acc[rows, :] = d
            else:
                acc[rows, :] += d

    def rope():
        pltpu.make_async_copy(trig_hbm, trig, lsem.at[1]).wait()

        @pl.when(away)
        def _():
            for k, b in enumerate((bq, bk, bv)):
                wait_recv(b, bsem.at[k])

        @pl.loop(0, SEQ // 128)
        def _(r):
            rows = pl.ds(pl.multiple_of(r * 128, 128), 128)
            here = trig[rows, :]
            other = pltpu.roll(here, HEAD // 2, 1)
            low = lax.broadcasted_iota(jnp.int32, (128, HEAD), 1) < HEAD // 2
            cs, sn = jnp.where(low, here, other), jnp.where(low, -other, here)
            for h in range(GROUP + 1):
                col = slice(h * HEAD, (h + 1) * HEAD)
                bias = bq[col][None, :] if h < GROUP else bk[...]
                t = acc[rows, col] + bias
                t = (t * cs + pltpu.roll(t, HEAD // 2, 1) * sn).astype(BF16)
                if h < GROUP:
                    qb[rows, col] = t
                else:
                    kb[rows, :] = t
            vb[rows, :] = (acc[rows, QC + HEAD :] + bv[...]).astype(BF16)

    scale = float(np.log2(np.e)) / float(np.sqrt(HEAD))
    QB = 256

    def attend(i, lo, hi):
        n = (i + 1) * QB

        @pl.loop(lo, hi, unroll=hi - lo)
        def _(h):
            col = pl.ds(pl.multiple_of(h * HEAD, HEAD), HEAD)
            q = qb[i * QB : n, col]
            near, far = slice(i * QB, n), slice(0, i * QB)

            def score(part):
                return lax.dot_general(q, kb[part, :], (((1,), (1,)), ((), ())), preferred_element_type=F32)

            qi = lax.broadcasted_iota(jnp.int32, (QB, QB), 0)
            ki = lax.broadcasted_iota(jnp.int32, (QB, QB), 1)
            parts = [(near, jnp.where(qi >= ki, score(near), -1e30))] + ([(far, score(far))] if i else [])
            top = functools.reduce(jnp.maximum, [jnp.max(sc, axis=-1, keepdims=True) for _, sc in parts])
            tot, o = 0.0, 0.0
            for part, sc in parts:
                w = jnp.exp2((sc - top) * scale)
                tot += jnp.sum(w, axis=-1, keepdims=True)
                o += jnp.dot(w.astype(BF16), vb[part, :], preferred_element_type=F32)
            hb[near, col] = (o / tot).astype(BF16)

    def st(r0, nr, j):
        return xb.at[pl.ds(r0, nr), pl.ds(j * OC, OC)]

    def out_at(j):
        return feature_block(j // 2, j % 2)

    def terms(st_, j):
        wrow = pl.ds(pl.multiple_of(out_at(j), 128), OC)

        @pl.loop(0, 2)
        def _(r):
            rows = pl.ds(pl.multiple_of(st_ * 512 + r * 256, 256), 256)
            acc[rows, pl.ds(0, OC)] = lax.dot_general(
                hb[rows, :], wob[wrow, :], (((1,), (1,)), ((), ())), preferred_element_type=F32
            )

        @pl.when(c != st_)
        def _():
            @pl.loop(0, 8)
            def _(r):
                r0 = pl.multiple_of(r * 64, 64)
                xb[pl.ds(r0, 64), pl.ds(j * OC, OC)] = acc[pl.ds(st_ * 512 + r0, 64), pl.ds(0, OC)].astype(BF16)

            send(remote(lambda: (st(0, 512, j), prcv.at[j], psem.at[j]), SIB), cores[1 - st_])

    def pair(st_, j, mine_):
        wait_recv(prcv.at[j], psem.at[j])
        oc = pl.ds(j * OC, OC)

        def total(x_, h):
            r0 = x_ * ROWS + h * half_rows
            mine = acc[pl.ds(pl.multiple_of(st_ * 512 + r0, 64), half_rows), pl.ds(0, OC)]
            return mine + prcv[j, pl.ds(pl.multiple_of(r0, 64), half_rows), :].astype(F32)

        for h in (0, 1):
            xb[512 + h * 64 : 576 + h * 64, oc] = total(x2, h).astype(BF16)
        send(remote(lambda: (st(512, 64, j), r1.at[j, 0], r1sem.at[j, 0]), XP), mine_)
        send(remote(lambda: (st(576, 64, j), r1.at[j, 1], r1sem.at[j, 1]), XM), mine_)
        xb[704:768, oc] = total(xp, 1).astype(BF16)
        xb[768:832, oc] = total(xm, 0).astype(BF16)
        send(remote(lambda: (st(704, 64, j), r2.at[j, 1], r2sem.at[j, 1]), XP), mine_)
        send(remote(lambda: (st(768, 64, j), r2.at[j, 2], r2sem.at[j, 2]), XM), mine_)
        held[j, 0] = total(xp, 0)
        held[j, 1] = total(xm, 1)
        held[j, 2] = total(x, 0)
        held[j, 3] = total(x, 1)

    def relay(st_, j, mine_):
        oc = pl.ds(j * OC, OC)
        wait_recv(r1.at[j, 0], r1sem.at[j, 0])
        xb[640:704, oc] = (held[j, 0] + r1[j, 0].astype(F32)).astype(BF16)
        send(remote(lambda: (st(640, 64, j), r2.at[j, 0], r2sem.at[j, 0]), XP), mine_)
        wait_recv(r1.at[j, 1], r1sem.at[j, 1])
        xb[832:896, oc] = (held[j, 1] + r1[j, 1].astype(F32)).astype(BF16)
        send(remote(lambda: (st(832, 64, j), r2.at[j, 3], r2sem.at[j, 3]), XM), mine_)

    def out_cols(j):
        return pl.ds(pl.multiple_of(out_at(j), 128), OC)

    def final(st_, j, mine_):
        oc = pl.ds(j * OC, OC)
        for k in range(4):
            wait_recv(r2.at[j, k], r2sem.at[j, k])

        def whole(h):
            return (held[j, 2 + h] + r2[j, h].astype(F32) + r2[j, 2 + h].astype(F32)).astype(BF16)

        @pl.when(home)
        def _():
            for h in (0, 1):
                out[h * 64 : h * 64 + 64, out_cols(j)] = whole(h)

        @pl.when(away)
        def _():
            for h in (0, 1):
                xb[896 + h * 64 : 960 + h * 64, oc] = whole(h)
            send(remote(lambda: (st(896, 128, j), out.at[:, out_cols(j)], fsem.at[j]), SWAP), aways[st_])

    def ring(fn, st_, j):
        pl.when(cores[st_])(lambda: fn(st_, j, cores[st_]))

    for tok_ in SCHEDULE:
        kind, arg = tok_[0], tok_[1:]
        token[0] = kind
        if kind == "x":
            {"w": x_swap, "o": x_own, "r": x_relay, "l": x_last, "s": x_sib}[arg[0]](*map(int, arg[1:]))
        elif kind in "qw" and arg == "o":
            place_own(parts_of[kind], qkv if kind == "q" else wout)
        elif kind in "qw" and arg == "s":
            place_sib(parts_of[kind], qkv if kind == "q" else wout)
        elif kind in "qw":
            (qkv if kind == "q" else wout).step(arg)
        elif kind == "p":
            project(*map(int, arg))
        elif kind == "n":
            norm()
        elif kind == "e":
            rope()
        elif kind == "a":
            attend(*map(int, arg))
        elif kind == "d":
            wait_sends(True)
        elif kind == "t":
            terms(*map(int, arg))
        else:
            ring({"g": pair, "r": relay, "f": final}[kind], *map(int, arg))

    @pl.when(away)
    def _():
        for j in range(NO):
            wait_recv(out.at[:, out_cols(j)], fsem.at[j])

    wait_sends(False)
    assert len(sends) <= N_SEND, len(sends)


def body(tokens, gain, wq, wk, wv, bq, bk, bv, wo):
    trig = rope_tables()
    any_, vm = pl.BlockSpec(memory_space=pl.ANY), pl.BlockSpec(memory_space=pltpu.VMEM)
    dma = lambda *n: pltpu.SemaphoreType.DMA(n)
    return pl.pallas_call(
        kernel,
        out_shape=jax.ShapeDtypeStruct((ROWS, WIDTH), BF16),
        in_specs=[any_, vm, any_, any_, any_, vm, vm, vm, any_, any_],
        out_specs=vm,
        scratch_shapes=[
            pltpu.VMEM((ROWS, WIDTH), BF16),
            pltpu.VMEM((ROWS, WIDTH), BF16),
            pltpu.VMEM((SEQ, WIDTH), BF16),
            pltpu.VMEM((WIDTH, WC), BF16),
            pltpu.VMEM((WIDTH, QC), BF16),
            pltpu.VMEM((SEQ, WC), F32),
            pltpu.VMEM((SEQ, QC), BF16),
            pltpu.VMEM((SEQ, HEAD), BF16),
            pltpu.VMEM((SEQ, HEAD), BF16),
            pltpu.VMEM((SEQ, QC), BF16),
            pltpu.VMEM((SEQ, HEAD), F32),
            pltpu.VMEM((QC,), F32),
            pltpu.VMEM((1, HEAD), F32),
            pltpu.VMEM((1, HEAD), F32),
            pltpu.VMEM((NO, 512, OC), BF16),
            pltpu.VMEM((NO, 2, 64, OC), BF16),
            pltpu.VMEM((NO, 4, 64, OC), BF16),
            pltpu.VMEM((NO, 4, 64, OC), F32),
            dma(8), dma(N_SEND), dma(16, 2), dma(16, 2), dma(4), dma(NK, 4), dma(NK, 4), dma(NK), dma(3),
            dma(NO), dma(NO, 2), dma(NO, 4), dma(NO),
        ],
        compiler_params=pltpu.CompilerParams(
            collective_id=0, has_side_effects=True, vmem_limit_bytes=67043328
        ),
    )(
        tokens, gain.reshape(1, -1), wq, wk, wv, bq, bk.reshape(1, -1), bv.reshape(1, -1), wo,
        jnp.asarray(trig),
    )


def solution(mesh):
    placed = (
        P(("fsdp", "sp"), None), P(), P("fsdp", "sp"), P("fsdp", "sp"), P("fsdp", "sp"),
        P("sp"), P("sp"), P("sp"), P("fsdp", "sp"),
    )
    return jax.shard_map(
        body, mesh=mesh, in_specs=placed, out_specs=P(("fsdp", "sp"), None), check_vma=False
    )
```

```python
import functools

import jax
import jax.numpy as jnp
import numpy as np
from jax import lax
from jax.experimental import pallas as pl
from jax.experimental.pallas import tpu as pltpu
from jax.sharding import PartitionSpec as P

MESH = pl.DeviceIdType.MESH
WIDTH = 5120
HEAD = 128
GROUP = 5
QC = GROUP * HEAD
WC = QC + 2 * HEAD
SEQ = 1024
ROWS = 128
WR = 320
HR = WR // 2
KC = 1280
NK = WIDTH // KC
OC = 640
NO = WIDTH // OC
N_SEND = 300
F32 = jnp.float32
BF16 = jnp.bfloat16
LATE_Q, OUTER_Q = 0, (0, 1)
LATE_O, OUTER_O = 1, (0, 2, 3)
SCHEDULE = (
    "qo", "n", "qn1", "xw", "xo0", "qs", "qn2", "xo1", "xo2", "qh1", "xr0", "qn4a", "qh2", "xr1", "xr2", "xo3",
    "qh3", "qn3b", "wo", "qh4", "xl0", "xs0", "qn4b", "qh4b", "qn3a", "xl2", "p00", "xl1", "xr3", "ws", "p01", "xs2",
    "p20", "qh6", "xs1", "qn5", "wh1", "qh5", "p11", "xl3", "p10", "qn6b", "wh2", "p21", "qh7a", "xs3", "qn6a", "p30",
    "wn1", "qh7b", "qh8", "p31", "e", "d", "a202", "wn2", "a325", "wh3", "a302", "a225", "t10", "a005", "a105", "t00",
    "g00", "wn4a", "g10", "wn3a", "wn4b", "t02", "wh7a", "r10", "t12", "g12", "wh4b", "t14", "wh4", "g14", "g02", "wn3b",
    "t11", "r00", "wn5", "t04", "g11", "r02", "wn6a", "t16", "f00", "g04", "t01", "g01", "t06", "g06", "f02", "f10",
    "wh6", "wh5", "t03", "r14", "r12", "g16", "wh8", "wn6b", "t13", "r04", "g13", "t15", "g15", "f14", "r01", "g03",
    "t05", "wh7b", "t17", "f12", "g17", "f04", "f01", "r03", "g05", "t07", "g07", "r16", "r06", "r13", "r17", "f16",
    "r15", "f03", "r11", "f13", "r05", "r07", "f17", "f15", "f06", "f05", "f07", "f11",
)


def rope_tables():
    half = HEAD // 2
    freq = np.float32(1000000.0) ** (-(np.arange(half, dtype=np.float32) * 2.0 / HEAD)).astype(np.float32)
    angle = (np.arange(SEQ, dtype=np.float32)[:, None] * freq[None, :]).astype(np.float64)
    cos = np.cos(angle).astype(np.float32)
    sin = np.sin(angle).astype(np.float32)
    return np.concatenate([cos, sin], 1)


def kernel(
    tok_hbm, gain, wq_hbm, wk_hbm, wv_hbm, bq_in, bk_in, bv_in, wo_hbm, trig_hbm,
    out,
    tok, stage, xb, wb, wob, acc, qb, kb, vb, hb, trig, bq, bk, bv,
    prcv, r1, r2, held,
    lsem, ssem, wsem, wosem, wsib, xsem, xsib, swsem, bsem, psem, r1sem, r2sem, fsem,
):
    f = lax.axis_index("fsdp")
    s = lax.axis_index("sp")
    c = f % 2
    zh = (f // 2) % 2
    y = f // 4
    zl = s // 4
    x = s % 4
    z = zh * 2 + zl
    home = c == zl
    away = c != zl
    cores = (c == 0, c == 1)
    aways = ((c == 0) & away, (c == 1) & away)
    yp, ym, y2 = (y + 1) % 4, (y + 3) % 4, (y + 2) % 4
    zp, zm, z2 = (z + 1) % 4, (z + 3) % 4, (z + 2) % 4
    xp, xm, x2 = (x + 1) % 4, (x + 3) % 4, (x + 2) % 4

    def dev(y_, z_, x_, c_):
        return ((y_ * 2 + z_ // 2) * 2 + c_, (z_ % 2) * 4 + x_)

    YP, YM = dev(yp, z, x, c), dev(ym, z, x, c)
    ZP, ZM = dev(y, zp, x, c), dev(y, zm, x, c)
    XP, XM = dev(y, z, xp, c), dev(y, z, xm, c)
    SIB = dev(y, z, x, 1 - c)
    SWAP = dev(y, zh * 2 + c, x, zl)

    sends, token = [], [None]

    def send(mk, cond=None):
        k = len(sends)
        mk(ssem.at[k]).start()
        sends.append((cond, mk, token[0]))

    def wait_sends(of_tokens):
        for cond in (None, home, away, *cores, *aways):
            group = [(k, e[1]) for k, e in enumerate(sends) if e[0] is cond and (e[2] == "x") == of_tokens]
            if not group:
                continue

            def drain(group=group):
                for k, mk in group:
                    mk(ssem.at[k]).wait_send()

            if cond is None:
                drain()
            else:
                pl.when(cond)(drain)

    def remote(refs, to):
        def mk(sem):
            src, dst, rsem = refs()
            return pltpu.make_async_remote_copy(
                src_ref=src, dst_ref=dst, send_sem=sem, recv_sem=rsem, device_id=to, device_id_type=MESH
            )

        return mk

    def wait_recv(dst, rsem):
        pltpu.make_async_remote_copy(
            src_ref=dst, dst_ref=dst, send_sem=ssem.at[0], recv_sem=rsem, device_id=SIB, device_id_type=MESH
        ).wait_recv()

    pltpu.make_async_copy(tok_hbm, tok, lsem.at[0]).start()
    barrier = pltpu.get_barrier_semaphore()
    for peer in (YP, YM, ZP, ZM, XP, XM, SIB):
        pl.semaphore_signal(barrier, inc=1, device_id=peer, device_id_type=MESH)

    @pl.when(away)
    def _():
        pl.semaphore_signal(barrier, inc=1, device_id=SWAP, device_id_type=MESH)

    pltpu.make_async_copy(trig_hbm, trig, lsem.at[1]).start()

    def block(y_, z_, i):
        return (y_, z_, i)

    def index_of(b):
        return 4 * b[0] + 2 * (b[1] // 2) + b[2]

    own_f = index_of((y, z, c))
    sib_f = index_of((y, z, 1 - c))

    def own_rows(buf, f_):
        return buf.at[pl.ds(pl.multiple_of(f_ * WR, 32), WR)]

    local_parts = (
        (wq_hbm, wb, 0, QC), (wk_hbm, wb, QC, HEAD), (wv_hbm, wb, QC + HEAD, HEAD), (wo_hbm, wob, 0, QC),
    )

    def part_view(buf, f_, col, n):
        return buf.at[pl.ds(pl.multiple_of(f_ * WR, 32), WR), pl.ds(col, n)]

    @pl.when(home)
    def _():
        for k, (src, buf, col, n) in enumerate(local_parts):
            pltpu.make_async_copy(src, part_view(buf, own_f, col, n), lsem.at[3 + k]).start()
        for k, (src, dst) in enumerate(((bq_in, bq), (bk_in, bk), (bv_in, bv))):
            dst[...] = src[...]

    my_rows = pl.multiple_of(c * (4 * ROWS) + x * ROWS, ROWS)

    def norm_to(dst, base):
        @pl.loop(0, ROWS // 16)
        def _(r):
            r0 = pl.multiple_of(r * 16, 16)
            t = tok[pl.ds(r0, 16), :].astype(F32)
            ms = jnp.mean(t * t, axis=-1, keepdims=True)
            dst[pl.ds(pl.multiple_of(base + r0, 16), 16), :] = (t * lax.rsqrt(ms + 1e-06) * gain[...]).astype(BF16)

    def norm():
        pltpu.make_async_copy(tok_hbm, tok, lsem.at[0]).wait()

        @pl.when(home)
        def _():
            norm_to(xb, my_rows)

        @pl.when(away)
        def _():
            norm_to(stage, 0)

    pl.semaphore_wait(barrier, 7 + (c + zl) % 2)

    zq, zn = z + 1 - 2 * zl, (z + 3 + 2 * zl) % 4
    ZN = dev(y, zn, x, c)

    class Flow:
        def __init__(self, buf, rsem, late, outer):
            self.buf, self.rsem = buf, rsem
            self.own = [(0, 0), (0, 1)]
            self.sib = [(1, 0), (1, 1)]
            self.zfirst = self.sib + self.own[2 - late :]
            self.yfirst = self.own[: 2 - late]
            self.outer = outer

        def refs(self, y_, z_, u):
            k = 4 * y_ + 2 * (z_ // 2) + (c + u[0]) % 2
            v = self.buf.at[pl.ds(pl.multiple_of(k * WR + u[1] * HR, 32), HR)]
            return v, v, self.rsem.at[k, u[1]]

        def fwd(self, y_, z_, u, to, cond):
            send(remote(lambda: self.refs(y_, z_, u), to), cond)

        def wait(self, y_, z_, units):
            for u in units:
                _, v, sem = self.refs(y_, z_, u)
                wait_recv(v, sem)

        def spread(self, y_, z_, units, dirs, cond):
            for u in units:
                for to in dirs:
                    self.fwd(y_, z_, u, to, cond)

        def relay_y(self, z_, units, flip, cond):
            for n, u in enumerate(units):
                for y_, to, turn in ((ym, YP, 0), (yp, YM, 1)):
                    self.wait(y_, z_, [u])
                    if (n + flip) % 2 == turn:
                        self.fwd(y_, z_, u, to, cond)

        def relay_z(self, y_, units, row, cond):
            for n, u in enumerate(units):
                if row in self.outer:
                    self.wait(y_, zq, [u])
                    self.fwd(y_, zq, u, ZN, cond)
                    self.wait(y_, zn, [u])
                    continue
                for z_, to, turn in ((zm, ZP, 0), (zp, ZM, 1)):
                    self.wait(y_, z_, [u])
                    if n % 2 == turn:
                        self.fwd(y_, z_, u, to, cond)

        def h0(self):
            for u in self.own:
                self.spread(y, z, [u], (YP, YM, ZP, ZM), home)

        def h0s(self):
            for u in self.sib:
                self.spread(y, z, [u], (ZP, ZM, YP, YM), home)

        def h1(self):
            self.relay_y(z, self.yfirst, 0, home)
            self.spread(ym, z, self.yfirst, (ZP, ZM), home)
            self.spread(yp, z, self.yfirst, (ZP, ZM), home)

        def h2(self):
            self.relay_y(z, self.zfirst, len(self.yfirst), home)

        def h3(self):
            self.wait(y2, z, self.yfirst)
            self.spread(y2, z, self.yfirst, (ZP, ZM), home)

        def h4(self):
            for u in self.zfirst[::-1]:
                self.wait(y, z2, [u])
                self.spread(y, z2, [u], (YP, YM), home)

        def h4b(self):
            self.wait(y, z2, self.yfirst)

        def h5(self):
            self.relay_y(z2, self.zfirst[::-1], 0, home)

        def h6(self):
            self.wait(ym, z2, self.yfirst)
            self.wait(yp, z2, self.yfirst)

        def h7a(self):
            self.wait(y2, z, self.zfirst)

        def h7b(self):
            self.wait(y2, z2, self.zfirst)

        def h8(self):
            self.wait(y2, z2, self.yfirst)

        def n1(self):
            self.relay_z(y, self.own, 0, away)
            u = self.own[2 - len(self.zfirst) + 2 :]
            for v in u:
                for z_ in (zm, zp):
                    self.spread(y, z_, [v], (YP, YM), away)

        def n2(self):
            self.relay_z(y, self.sib, 1, away)
            for v in self.sib:
                for z_ in (zm, zp):
                    self.spread(y, z_, [v], (YP, YM), away)

        def n3a(self):
            self.relay_y(zq, self.order_n(), 0, away)

        def n3b(self):
            self.relay_y(zn, self.order_n(), 1, away)

        def order_n(self):
            return [u for u in self.zfirst if u[0] == 0] + self.sib

        def n4a(self):
            self.relay_z(ym, self.yfirst, 2, away)

        def n4b(self):
            self.relay_z(yp, self.yfirst, 3, away)

        def n5(self):
            self.relay_z(y2, self.yfirst, 4, away)

        def n6a(self):
            self.wait(y2, zq, self.zfirst)

        def n6b(self):
            self.wait(y2, zn, self.zfirst)

        def step(self, name):
            @pl.when(home if name[0] == "h" else away)
            def _():
                getattr(self, name)()

    qkv = Flow(wb, wsem, LATE_Q, OUTER_Q)
    wout = Flow(wob, wosem, LATE_O, OUTER_O)

    def place_own(parts, flow):
        @pl.when(away)
        def _():
            for k, (src, buf, col, n) in parts:
                send(remote(lambda a=src, b=buf, o=col, m=n, k=k: (a, part_view(b, own_f, o, m), wsib.at[k]), SIB), away)

        @pl.when(home)
        def _():
            for k, (src, buf, col, n) in parts:
                pltpu.make_async_copy(src, part_view(buf, own_f, col, n), lsem.at[3 + k]).wait()
            flow.h0()

    def place_sib(parts, flow):
        @pl.when(home)
        def _():
            for k, (src, buf, col, n) in parts:
                wait_recv(part_view(buf, sib_f, col, n), wsib.at[k])
            flow.h0s()

    parts_of = {"q": list(enumerate(local_parts))[:3], "w": list(enumerate(local_parts))[3:]}

    chunk_at = (y, yp, ym, y2)

    def xv(core, x_, kk, r0=0, nr=ROWS):
        return xb.at[
            pl.ds(pl.multiple_of(core * (4 * ROWS) + x_ * ROWS + r0, 16), nr),
            pl.ds(pl.multiple_of(chunk_at[kk] * KC, 128), KC),
        ]

    def x_swap():
        @pl.when(away)
        def _():
            for kk in range(NK):
                send(remote(lambda kk=kk: (
                    stage.at[:, pl.ds(pl.multiple_of(chunk_at[kk] * KC, 128), KC)], xv(1 - c, x, kk), swsem.at[kk]
                ), SWAP), away)
                if kk == 0:
                    for k, (a, b) in enumerate(((bq_in, bq), (bk_in, bk), (bv_in, bv))):
                        send(remote(lambda a=a, b=b, k=k: (a, b, bsem.at[k]), SWAP), away)

    half_rows = ROWS // 2

    def xsend(where, sem, to):
        def refs():
            v = xv(*where)
            return v, v, sem

        send(remote(refs, to))

    def x_own(kk):
        @pl.when(away)
        def _():
            wait_recv(xv(c, x, kk), swsem.at[kk])

        xsend((c, x, kk), xsem.at[kk, 0], XP)
        xsend((c, x, kk), xsem.at[kk, 1], XM)
        xsend((c, x, kk), xsib.at[kk, 0], SIB)

    def x_relay(kk):
        wait_recv(xv(c, xm, kk), xsem.at[kk, 0])
        xsend((c, xm, kk, 0, half_rows), xsem.at[kk, 2], XP)
        wait_recv(xv(c, xp, kk), xsem.at[kk, 1])
        xsend((c, xp, kk, half_rows, half_rows), xsem.at[kk, 3], XM)
        xsend((c, xm, kk), xsib.at[kk, 1], SIB)
        xsend((c, xp, kk), xsib.at[kk, 2], SIB)

    def x_last(kk):
        wait_recv(xv(c, x2, kk, 0, half_rows), xsem.at[kk, 2])
        wait_recv(xv(c, x2, kk, half_rows, half_rows), xsem.at[kk, 3])
        xsend((c, x2, kk), xsib.at[kk, 3], SIB)

    def x_sib(kk):
        for k, x_ in enumerate((x, xm, xp, x2)):
            wait_recv(xv(1 - c, x_, kk), xsib.at[kk, k])

    RB = 256

    def feature_block(kk, side):
        return (chunk_at[kk] * 2 + (zh + side) % 2) * OC

    started = []

    def project(kk, side):
        cols = pl.ds(pl.multiple_of(feature_block(kk, side), 128), OC)
        first = not started
        started.append(kk)

        @pl.loop(0, SEQ // RB)
        def _(r):
            rows = pl.ds(pl.multiple_of(r * RB, RB), RB)
            d = jnp.dot(xb[rows, cols], wb[cols, :], preferred_element_type=F32)
            if first:
                acc[rows, :] = d
            else:
                acc[rows, :] += d

    def rope():
        pltpu.make_async_copy(trig_hbm, trig, lsem.at[1]).wait()

        @pl.when(away)
        def _():
            for k, b in enumerate((bq, bk, bv)):
                wait_recv(b, bsem.at[k])

        @pl.loop(0, SEQ // 128)
        def _(r):
            rows = pl.ds(pl.multiple_of(r * 128, 128), 128)
            here = trig[rows, :]
            other = pltpu.roll(here, HEAD // 2, 1)
            low = lax.broadcasted_iota(jnp.int32, (128, HEAD), 1) < HEAD // 2
            cs, sn = jnp.where(low, here, other), jnp.where(low, -other, here)
            for h in range(GROUP + 1):
                col = slice(h * HEAD, (h + 1) * HEAD)
                bias = bq[col][None, :] if h < GROUP else bk[...]
                t = acc[rows, col] + bias
                t = (t * cs + pltpu.roll(t, HEAD // 2, 1) * sn).astype(BF16)
                if h < GROUP:
                    qb[rows, col] = t
                else:
                    kb[rows, :] = t
            vb[rows, :] = (acc[rows, QC + HEAD :] + bv[...]).astype(BF16)

    scale = float(np.log2(np.e)) / float(np.sqrt(HEAD))
    QB = 256

    def attend(i, lo, hi):
        n = (i + 1) * QB

        @pl.loop(lo, hi, unroll=hi - lo)
        def _(h):
            col = pl.ds(pl.multiple_of(h * HEAD, HEAD), HEAD)
            q = qb[i * QB : n, col]
            near, far = slice(i * QB, n), slice(0, i * QB)

            def score(part):
                return lax.dot_general(q, kb[part, :], (((1,), (1,)), ((), ())), preferred_element_type=F32)

            qi = lax.broadcasted_iota(jnp.int32, (QB, QB), 0)
            ki = lax.broadcasted_iota(jnp.int32, (QB, QB), 1)
            parts = [(near, jnp.where(qi >= ki, score(near), -1e30))] + ([(far, score(far))] if i else [])
            top = functools.reduce(jnp.maximum, [jnp.max(sc, axis=-1, keepdims=True) for _, sc in parts])
            tot, o = 0.0, 0.0
            for part, sc in parts:
                w = jnp.exp2((sc - top) * scale)
                tot += jnp.sum(w, axis=-1, keepdims=True)
                o += jnp.dot(w.astype(BF16), vb[part, :], preferred_element_type=F32)
            hb[near, col] = (o / tot).astype(BF16)

    def st(r0, nr, j):
        return xb.at[pl.ds(r0, nr), pl.ds(j * OC, OC)]

    def out_at(j):
        return feature_block(j // 2, j % 2)

    def terms(st_, j):
        wrow = pl.ds(pl.multiple_of(out_at(j), 128), OC)

        @pl.loop(0, 2)
        def _(r):
            rows = pl.ds(pl.multiple_of(st_ * 512 + r * 256, 256), 256)
            acc[rows, pl.ds(0, OC)] = lax.dot_general(
                hb[rows, :], wob[wrow, :], (((1,), (1,)), ((), ())), preferred_element_type=F32
            )

        @pl.when(c != st_)
        def _():
            @pl.loop(0, 8)
            def _(r):
                r0 = pl.multiple_of(r * 64, 64)
                xb[pl.ds(r0, 64), pl.ds(j * OC, OC)] = acc[pl.ds(st_ * 512 + r0, 64), pl.ds(0, OC)].astype(BF16)

            send(remote(lambda: (st(0, 512, j), prcv.at[j], psem.at[j]), SIB), cores[1 - st_])

    def pair(st_, j, mine_):
        wait_recv(prcv.at[j], psem.at[j])
        oc = pl.ds(j * OC, OC)

        def total(x_, h):
            r0 = x_ * ROWS + h * half_rows
            mine = acc[pl.ds(pl.multiple_of(st_ * 512 + r0, 64), half_rows), pl.ds(0, OC)]
            return mine + prcv[j, pl.ds(pl.multiple_of(r0, 64), half_rows), :].astype(F32)

        for h in (0, 1):
            xb[512 + h * 64 : 576 + h * 64, oc] = total(x2, h).astype(BF16)
        send(remote(lambda: (st(512, 64, j), r1.at[j, 0], r1sem.at[j, 0]), XP), mine_)
        send(remote(lambda: (st(576, 64, j), r1.at[j, 1], r1sem.at[j, 1]), XM), mine_)
        xb[704:768, oc] = total(xp, 1).astype(BF16)
        xb[768:832, oc] = total(xm, 0).astype(BF16)
        send(remote(lambda: (st(704, 64, j), r2.at[j, 1], r2sem.at[j, 1]), XP), mine_)
        send(remote(lambda: (st(768, 64, j), r2.at[j, 2], r2sem.at[j, 2]), XM), mine_)
        held[j, 0] = total(xp, 0)
        held[j, 1] = total(xm, 1)
        held[j, 2] = total(x, 0)
        held[j, 3] = total(x, 1)

    def relay(st_, j, mine_):
        oc = pl.ds(j * OC, OC)
        wait_recv(r1.at[j, 0], r1sem.at[j, 0])
        xb[640:704, oc] = (held[j, 0] + r1[j, 0].astype(F32)).astype(BF16)
        send(remote(lambda: (st(640, 64, j), r2.at[j, 0], r2sem.at[j, 0]), XP), mine_)
        wait_recv(r1.at[j, 1], r1sem.at[j, 1])
        xb[832:896, oc] = (held[j, 1] + r1[j, 1].astype(F32)).astype(BF16)
        send(remote(lambda: (st(832, 64, j), r2.at[j, 3], r2sem.at[j, 3]), XM), mine_)

    def out_cols(j):
        return pl.ds(pl.multiple_of(out_at(j), 128), OC)

    def final(st_, j, mine_):
        oc = pl.ds(j * OC, OC)
        for k in range(4):
            wait_recv(r2.at[j, k], r2sem.at[j, k])

        def whole(h):
            return (held[j, 2 + h] + r2[j, h].astype(F32) + r2[j, 2 + h].astype(F32)).astype(BF16)

        @pl.when(home)
        def _():
            for h in (0, 1):
                out[h * 64 : h * 64 + 64, out_cols(j)] = whole(h)

        @pl.when(away)
        def _():
            for h in (0, 1):
                xb[896 + h * 64 : 960 + h * 64, oc] = whole(h)
            send(remote(lambda: (st(896, 128, j), out.at[:, out_cols(j)], fsem.at[j]), SWAP), aways[st_])

    def ring(fn, st_, j):
        pl.when(cores[st_])(lambda: fn(st_, j, cores[st_]))

    for tok_ in SCHEDULE:
        kind, arg = tok_[0], tok_[1:]
        token[0] = kind
        if kind == "x":
            {"w": x_swap, "o": x_own, "r": x_relay, "l": x_last, "s": x_sib}[arg[0]](*map(int, arg[1:]))
        elif kind in "qw" and arg == "o":
            place_own(parts_of[kind], qkv if kind == "q" else wout)
        elif kind in "qw" and arg == "s":
            place_sib(parts_of[kind], qkv if kind == "q" else wout)
        elif kind in "qw":
            (qkv if kind == "q" else wout).step(arg)
        elif kind == "p":
            project(*map(int, arg))
        elif kind == "n":
            norm()
        elif kind == "e":
            rope()
        elif kind == "a":
            attend(*map(int, arg))
        elif kind == "d":
            wait_sends(True)
        elif kind == "t":
            terms(*map(int, arg))
        else:
            ring({"g": pair, "r": relay, "f": final}[kind], *map(int, arg))

    @pl.when(away)
    def _():
        for j in range(NO):
            wait_recv(out.at[:, out_cols(j)], fsem.at[j])

    wait_sends(False)
    assert len(sends) <= N_SEND, len(sends)


def body(tokens, gain, wq, wk, wv, bq, bk, bv, wo):
    trig = rope_tables()
    any_, vm = pl.BlockSpec(memory_space=pl.ANY), pl.BlockSpec(memory_space=pltpu.VMEM)
    dma = lambda *n: pltpu.SemaphoreType.DMA(n)
    return pl.pallas_call(
        kernel,
        out_shape=jax.ShapeDtypeStruct((ROWS, WIDTH), BF16),
        in_specs=[any_, vm, any_, any_, any_, vm, vm, vm, any_, any_],
        out_specs=vm,
        scratch_shapes=[
            pltpu.VMEM((ROWS, WIDTH), BF16),
            pltpu.VMEM((ROWS, WIDTH), BF16),
            pltpu.VMEM((SEQ, WIDTH), BF16),
            pltpu.VMEM((WIDTH, WC), BF16),
            pltpu.VMEM((WIDTH, QC), BF16),
            pltpu.VMEM((SEQ, WC), F32),
            pltpu.VMEM((SEQ, QC), BF16),
            pltpu.VMEM((SEQ, HEAD), BF16),
            pltpu.VMEM((SEQ, HEAD), BF16),
            pltpu.VMEM((SEQ, QC), BF16),
            pltpu.VMEM((SEQ, HEAD), F32),
            pltpu.VMEM((QC,), F32),
            pltpu.VMEM((1, HEAD), F32),
            pltpu.VMEM((1, HEAD), F32),
            pltpu.VMEM((NO, 512, OC), BF16),
            pltpu.VMEM((NO, 2, 64, OC), BF16),
            pltpu.VMEM((NO, 4, 64, OC), BF16),
            pltpu.VMEM((NO, 4, 64, OC), F32),
            dma(8), dma(N_SEND), dma(16, 2), dma(16, 2), dma(4), dma(NK, 4), dma(NK, 4), dma(NK), dma(3),
            dma(NO), dma(NO, 2), dma(NO, 4), dma(NO),
        ],
        compiler_params=pltpu.CompilerParams(
            collective_id=0, has_side_effects=True, vmem_limit_bytes=67043328
        ),
    )(
        tokens, gain.reshape(1, -1), wq, wk, wv, bq, bk.reshape(1, -1), bv.reshape(1, -1), wo,
        jnp.asarray(trig),
    )


def solution(mesh):
    placed = (
        P(("fsdp", "sp"), None), P(), P("fsdp", "sp"), P("fsdp", "sp"), P("fsdp", "sp"),
        P("sp"), P("sp"), P("sp"), P("fsdp", "sp"),
    )
    return jax.shard_map(
        body, mesh=mesh, in_specs=placed, out_specs=P(("fsdp", "sp"), None), check_vma=False
    )
```
